1024 devices in a mesh: pp: 4 (over y_hi), fsdp: 64 (over x, z), tp: 4 (over y_lo, core).
Axes of the slice: x: 8, y: 8 (y_hi: 4, y_lo: 2; y = y_hi * 2 + y_lo), z: 8, core: 2. Of those that a mesh axis runs over, the one named last changes fastest.
Arguments:
- saved_inputs: bfloat16 [4, 8192, 8192], P('pp', 'fsdp', 'tp'), may hold values from -6 to 6
- returned: bfloat16 [4, 8192, 8192], P('pp', 'fsdp', 'tp'), may hold values from -6 to 6
- proj_weight: bfloat16 [4, 8192, 640], P('pp', 'tp', 'fsdp'), may hold values from -0.03125 to 0.03125
- log_rate: float32 [4, 128], P('pp', 'tp'), may hold values from -4.6 to -1.2
- step_bias: float32 [4, 128], P('pp', 'tp'), may hold values from -3 to -1
- skip_gain: float32 [4, 128], P('pp', 'tp'), may hold values from 0.5 to 1.5
Outputs:
- grad_out: bfloat16 [4, 8192, 8192], P('pp', 'fsdp', 'tp')
- weight_grad: float32 [4, 8192, 640], P('pp', 'tp', 'fsdp')
The draws below stay inside these ranges and needn't reach their ends.
All inputs are finite; a program needn't handle non-finite values.
Results may differ from the reference program's by a relative error of at most 0.0044.
Values may be sent and summed in bfloat16 or wider, within the bound.
No kernel may reach another device: no remote copies, remote signals or barrier semaphores. Data moves between devices by JAX's collectives and lax.ppermute only.
A program may use at most 64 MiB of HBM per device.

```python
import jax
import jax.numpy as jnp
from jax import lax

HEADS = 128
HEAD_DIM = 64
STATE = 256
BLOCK = 128
SEQ_LEN = 128
SECTIONS = 4
TOKENS = 8192
INNER = 8192
PCOLS = 640


def steps_of(key, shape, pieces, least, top_value):
    gain, own = 1.0, jax.random.fold_in(key, 6)
    for dim, parts in pieces:
        steps = jnp.exp(jax.random.uniform(jax.random.fold_in(own, dim), (parts,), jnp.float32, least / len(pieces), top_value / len(pieces)))
        gain = gain * jnp.repeat(steps, shape[dim] // parts).reshape([-1 if axis == dim else 1 for axis in range(len(shape))])
    return gain


def noise(own_key, dims, spread, reach, split=(), held_as=jnp.bfloat16):
    level = steps_of(own_key, dims, split, -0.22, 0.18) if split else 1.0
    result = jax.random.normal(own_key, dims, jnp.float32) * spread * level
    return jnp.minimum(jnp.maximum(result, -reach), reach).astype(held_as)


def setup_inputs(seed: int = 0) -> dict:
    keys = jax.random.split(jax.random.key(seed), 7)
    saved_inputs = noise(keys[0], (SECTIONS, TOKENS, INNER), 1.0, 6.0, ((0, 4), (1, 64), (2, 4)))
    returned = noise(keys[1], (SECTIONS, TOKENS, INNER), 1.0, 6.0, ((0, 4), (1, 64), (2, 4)))
    proj_weight = noise(keys[2], (SECTIONS, INNER, PCOLS), (4 * INNER) ** -0.5, 0.03125, ((0, 4), (1, 4), (2, 64)))
    log_rate = jnp.clip(-4.6 + 3.3999999 * jax.random.uniform(keys[3], (SECTIONS, HEADS), jnp.float32) ** steps_of(keys[3], (SECTIONS, HEADS), ((0, 4), (1, 4)), -0.2, 0.2), -4.6, -1.2)
    step_bias = jnp.clip(-3.0 + 2.0 * jax.random.uniform(keys[4], (SECTIONS, HEADS), jnp.float32) ** steps_of(keys[4], (SECTIONS, HEADS), ((0, 4), (1, 4)), -0.2, 0.2), -3.0, -1.0)
    skip_gain = jnp.clip(0.5 + 1.0 * jax.random.uniform(keys[5], (SECTIONS, HEADS), jnp.float32) ** steps_of(keys[5], (SECTIONS, HEADS), ((0, 4), (1, 4)), -0.2, 0.2), 0.5, 1.5)
    return {"saved_inputs": saved_inputs, "returned": returned, "proj_weight": proj_weight, "log_rate": log_rate, "step_bias": step_bias, "skip_gain": skip_gain}


def state_space(head_input, b_values, c_values, raw_step, log_rate, step_bias, skip_gain):
    length, head_count, head_size = head_input.shape
    blocks = length // BLOCK
    highest = lax.Precision.HIGHEST
    step_size = jax.nn.softplus(raw_step + step_bias[None, :])
    log_decay = -step_size * jnp.exp(log_rate)[None, :]
    block_values = head_input.reshape(blocks, BLOCK, head_count, head_size)
    b_blocks = b_values.reshape(blocks, BLOCK, b_values.shape[1])
    c_blocks = c_values.reshape(blocks, BLOCK, c_values.shape[1])
    cumulative = jnp.cumsum(log_decay.reshape(blocks, BLOCK, head_count), axis=1)
    scaled = block_values * step_size.reshape(blocks, BLOCK, head_count)[..., None]
    scores = jnp.einsum('kin,kjn->kij', c_blocks, b_blocks, precision=highest)
    causal = (jnp.arange(BLOCK)[:, None] >= jnp.arange(BLOCK)[None, :])[None, :, :, None]
    log_gaps = cumulative[:, :, None, :] - cumulative[:, None, :, :]
    mixing = jnp.where(causal, jnp.exp(jnp.where(causal, log_gaps, 0.0)), 0.0) * scores[..., None]
    within = jnp.einsum('kijh,kjhp->kihp', mixing, scaled, precision=highest)
    to_end = jnp.exp(cumulative[:, -1:, :] - cumulative)
    states = jnp.einsum('kjn,kjhp->khnp', b_blocks, scaled * to_end[..., None], precision=highest)
    totals = jnp.exp(cumulative[:, -1, :])

    def advance(running, inputs_pair):
        block_state, block_total = inputs_pair
        return (block_total[:, None, None] * running + block_state, running)
    start_state = jnp.zeros((head_count, b_values.shape[1], head_size), head_input.dtype)
    _, entering = lax.scan(advance, start_state, (states, totals))
    across = jnp.einsum('kin,khnp->kihp', c_blocks, entering, precision=highest) * jnp.exp(cumulative)[..., None]
    output = (within + across).reshape(length, head_count, head_size)
    return output + skip_gain[None, :, None] * head_input

def reference(saved_inputs, returned, proj_weight, log_rate, step_bias, skip_gain):
    incoming = jnp.roll(returned, -1, axis=0)

    def one_section(section_args):
        inputs, cotangent, weight, rates, biases, gains = section_args
        projected = jnp.dot(inputs, weight, preferred_element_type=jnp.float32)
        sequences = inputs.shape[0] // SEQ_LEN
        seq_inputs = inputs.astype(jnp.float32).reshape(sequences, SEQ_LEN, HEADS, HEAD_DIM)
        seq_proj = projected.reshape(sequences, SEQ_LEN, PCOLS)
        seq_cot = cotangent.astype(jnp.float32).reshape(sequences, SEQ_LEN, HEADS, HEAD_DIM)

        def per_sequence(triple):
            values, columns, upstream = triple

            def local_core(head_input, b_values, c_values, raw_step):
                return state_space(head_input, b_values, c_values, raw_step, rates, biases, gains)
            _, backward = jax.vjp(local_core, values, columns[:, :STATE], columns[:, STATE:2 * STATE], columns[:, 2 * STATE:])
            grad_x, grad_b, grad_c, grad_raw = backward(upstream)
            return (grad_x, jnp.concatenate([grad_b, grad_c, grad_raw], axis=1))
        grad_x, proj_grad = lax.map(per_sequence, (seq_inputs, seq_proj, seq_cot))
        proj_grad = proj_grad.reshape(inputs.shape[0], PCOLS).astype(jnp.bfloat16)
        back_proj = jnp.dot(proj_grad, weight.T, preferred_element_type=jnp.float32)
        grad_inputs = (cotangent.astype(jnp.float32) + grad_x.reshape(inputs.shape[0], INNER) + back_proj).astype(jnp.bfloat16)
        section_wgrad = jnp.dot(inputs.T, proj_grad, preferred_element_type=jnp.float32)
        return (grad_inputs, section_wgrad)
    grad_out, weight_grad = lax.map(one_section, (saved_inputs, incoming, proj_weight, log_rate, step_bias, skip_gain))
    return (grad_out, weight_grad)
```

```python
import jax
import jax.numpy as jnp
from jax import lax
from jax.experimental import pallas as pl
from jax.experimental.pallas import tpu as pltpu
from jax.sharding import PartitionSpec as P

HEAD_DIM = 64
STATE = 256
F32 = jnp.float32
BF16 = jnp.bfloat16
HIGHEST = lax.Precision.HIGHEST
NT = (((1,), (1,)), ((), ()))
NN = (((1,), (0,)), ((), ()))
VMEM_LIMIT = 56 * 1024 * 1024


def dot(a, b, dims=NN, precision=None):
    return lax.dot_general(a, b, dims, precision=precision, preferred_element_type=F32)


def call(kernel, outs, scratch=(), smem=(), inputs=0, name=None):
    specs = [
        pl.BlockSpec(memory_space=pltpu.SMEM if i in smem else pltpu.VMEM) for i in range(inputs)
    ]
    return pl.pallas_call(
        kernel,
        out_shape=outs,
        in_specs=specs,
        out_specs=jax.tree.map(lambda _: pl.BlockSpec(memory_space=pltpu.VMEM), outs),
        scratch_shapes=list(scratch),
        compiler_params=pltpu.CompilerParams(vmem_limit_bytes=VMEM_LIMIT),
        name=name,
    )


def project_kernel(w_ref, x_ref, out_ref, tail_ref):
    groups = w_ref.shape[0] // 8
    inner = x_ref.shape[1]
    quarter = inner // 4
    main = dot(w_ref[:, :inner], x_ref[...], NT)
    tail = None
    for q in range(4):
        tail_ref[...] = dot(w_ref[:, inner:], x_ref[:, q * quarter : (q + 1) * quarter], NT)
        part = tail_ref[pl.ds(q, 2 * groups, 4), :]
        tail = part if tail is None else tail + part
    for g in range(groups):
        out_ref[10 * g : 10 * g + 8, :] = main[8 * g : 8 * g + 8, :]
        out_ref[10 * g + 8 : 10 * g + 10, :] = tail[2 * g : 2 * g + 2, :]


def as_column(row):
    n = row.shape[1]
    at = lax.broadcasted_iota(jnp.int32, (n, n), 0) == lax.broadcasted_iota(jnp.int32, (n, n), 1)
    return jnp.sum(jnp.where(at, jnp.broadcast_to(row, (n, n)), 0.0), axis=1, keepdims=True)


def core_kernel(
    tp_ref, gain_ref, proj_ref, rate_ref, bias_ref, g_ref, x_ref,
    pack_ref, gx_ref,
    cum_ref, cols_ref, row_ref, col_ref, scores_ref,
):
    heads = rate_ref.shape[1]
    t = g_ref.shape[0]
    raw = proj_ref[pl.ds(pl.multiple_of(2 * STATE + tp_ref[0] * heads, heads), heads), :]
    z = raw + as_column(bias_ref[...])
    rate = as_column(jnp.exp(rate_ref[...]))
    step = jnp.maximum(z, 0.0) + jnp.log1p(jnp.exp(-jnp.abs(z)))
    first = lax.broadcasted_iota(jnp.int32, (t, t), 0)
    second = lax.broadcasted_iota(jnp.int32, (t, t), 1)
    cum = dot(-step * rate, jnp.where(first <= second, 1.0, 0.0), NN, HIGHEST)
    cum_ref[...] = cum
    cols_ref[...] = jnp.transpose(
        jnp.concatenate([cum, step, jnp.zeros((t - 2 * heads, t), F32)], axis=0)
    )
    scores = dot(jnp.transpose(proj_ref[:STATE, :]), proj_ref[STATE : 2 * STATE, :], NN, HIGHEST)
    causal = first <= second
    scores_ref[...] = jnp.where(causal, scores, 0.0)
    pack_ref[:t, :] = jnp.zeros((t, t), F32)
    left = second < HEAD_DIM

    def pair(k, carry):
        lanes = pl.ds(pl.multiple_of(k * 2 * HEAD_DIM, 2 * HEAD_DIM), 2 * HEAD_DIM)
        g = g_ref[:, lanes]
        x = x_ref[:, lanes]
        cols = cols_ref[...]
        none = jnp.zeros_like(g)
        gs = (jnp.where(left, g, none), jnp.where(left, none, g))
        moved = jnp.zeros((t, 2 * HEAD_DIM), F32)
        for a in range(2):
            h = 2 * k + a
            product = dot(x, gs[a], NT)
            step_col = cols[:, heads + a : heads + a + 1]
            decay = jnp.exp(jnp.minimum(cum_ref[pl.ds(h, 1), :] - cols[:, a : a + 1], 0.0))
            faded = product * decay
            stepped = faded * step_col
            pack_ref[:t, :] += stepped
            col_ref[...] = jnp.where(
                second == h,
                jnp.sum(faded * scores_ref[...], axis=1, keepdims=True),
                col_ref[...],
            )
            row_ref[pl.ds(h, 1), :] = jnp.sum(stepped * scores_ref[...], axis=0, keepdims=True)
            moved += dot((decay * scores_ref[...]).astype(BF16), gs[a], NN)
        step_both = jnp.where(left, cols[:, heads : heads + 1], cols[:, heads + 1 : heads + 2])
        gain = jnp.where(left, gain_ref[0, 2 * k], gain_ref[0, 2 * k + 1])
        up = g.astype(F32)
        gx_ref[:, lanes] = up + (moved * step_both + gain * up)
        cols_ref[...] = pltpu.roll(cols, t - 2, 1)
        return carry

    lax.fori_loop(0, heads // 2, pair, 0)
    pack_ref[:t, :] = jnp.where(causal, pack_ref[:t, :], 0.0)
    col = jnp.transpose(col_ref[...])[:heads, :]
    dcum = row_ref[...] - step * col
    decayed = dot(dcum, jnp.where(first >= second, 1.0, 0.0), NN, HIGHEST)
    pack_ref[t:, :] = (col - rate * decayed) * (1.0 / (1.0 + jnp.exp(-z)))


def grads_kernel(pack_ref, proj_ref, x_ref, out_ref, main_ref, tail_ref, wide_ref, grad_ref, rows_ref):
    parts, rows, t = pack_ref.shape
    heads = rows - t
    inner = x_ref.shape[1]
    quarter = inner // 4
    groups = out_ref.shape[0] // 8
    scores = pack_ref[0, :t, :]
    for p in range(1, parts):
        scores = scores + pack_ref[p, :t, :]
    grad_ref[:STATE, :] = dot(proj_ref[STATE : 2 * STATE, :], scores, NT, HIGHEST)
    grad_ref[STATE : 2 * STATE, :] = dot(proj_ref[:STATE, :], scores, NN, HIGHEST)
    for p in range(parts):
        grad_ref[2 * STATE + p * heads : 2 * STATE + (p + 1) * heads, :] = pack_ref[p, t:, :]
    for g in range(groups):
        rows_ref[8 * g : 8 * g + 8, :] = grad_ref[10 * g : 10 * g + 8, :]
        rows_ref[8 * groups + 2 * g : 8 * groups + 2 * g + 2, :] = grad_ref[10 * g + 8 : 10 * g + 10, :]
    main = rows_ref[: 8 * groups, :].astype(BF16)
    main_ref[...] = main
    out_ref[:, :inner] = dot(main, x_ref[...]).astype(BF16)
    for q in range(4):
        wide_ref[pl.ds(q, 2 * groups, 4), :] = rows_ref[8 * groups :, :]
    wide = wide_ref[...]
    quarter_of = lax.broadcasted_iota(jnp.int32, wide.shape, 0) % 4
    total = None
    for q in range(4):
        piece = jnp.where(quarter_of == q, wide, 0.0).astype(BF16)
        part = dot(piece, x_ref[:, q * quarter : (q + 1) * quarter])
        total = part if total is None else total + part
    out_ref[:, inner:] = total.astype(BF16)
    tail_ref[...] = wide.astype(BF16)


def back_kernel(main_ref, tail_ref, w_ref, gx_ref, out_ref):
    inner = gx_ref.shape[1]
    quarter = inner // 4
    main = jnp.transpose(main_ref[...].astype(F32)).astype(BF16)
    tail = jnp.transpose(tail_ref[...].astype(F32))
    quarter_of = lax.broadcasted_iota(jnp.int32, tail.shape, 1) % 4
    for q in range(4):
        lanes = slice(q * quarter, (q + 1) * quarter)
        piece = jnp.where(quarter_of == q, tail, 0.0).astype(BF16)
        back = dot(main, w_ref[:, lanes]) + dot(piece, w_ref[:, inner:])
        out_ref[:, lanes] = (gx_ref[:, lanes] + back).astype(BF16)


def per_device(saved_inputs, returned, proj_weight, log_rate, step_bias, skip_gain):
    x = saved_inputs[0]
    t, inner = x.shape
    heads = log_rate.shape[1]
    sections = lax.axis_size("pp")
    groups = lax.axis_size("fsdp")
    tps = lax.axis_size("tp")
    columns = proj_weight.shape[2]
    pcols = columns * groups
    wide = inner + 2 * inner // 8
    arrived = lax.ppermute(
        returned, "pp", [(i, (i - 1) % sections) for i in range(sections)]
    )[0]

    w = proj_weight[0].T
    shard = jnp.concatenate([w[:8], w[8:].reshape(8, inner // 4)], axis=1)
    gathered = lax.all_to_all(
        jnp.broadcast_to(shard[None], (groups, 8, wide)), "fsdp", 0, 0
    ).reshape(groups * 8, wide)

    partial = call(
        project_kernel,
        jax.ShapeDtypeStruct((pcols, t), F32),
        scratch=[pltpu.VMEM((groups * 8, t), F32)],
        inputs=2,
        name="project",
    )(gathered, x)
    share = lax.all_to_all(partial.reshape(tps, pcols // tps, t), "tp", 0, 0).sum(axis=0)
    proj = lax.all_gather(share, "tp", axis=0, tiled=True)

    pack, gx = call(
        core_kernel,
        (
            jax.ShapeDtypeStruct((t + heads, t), F32),
            jax.ShapeDtypeStruct((t, inner), F32),
        ),
        scratch=[
            pltpu.VMEM((heads, t), F32),
            pltpu.VMEM((t, t), F32),
            pltpu.VMEM((heads, t), F32),
            pltpu.VMEM((t, t), F32),
            pltpu.VMEM((t, t), F32),
        ],
        smem=(0, 1),
        inputs=7,
        name="core",
    )(lax.axis_index("tp").reshape(1), skip_gain, proj, log_rate, step_bias, arrived, x)

    packs = lax.all_gather(pack, "tp", axis=0)
    contrib, main, tail = call(
        grads_kernel,
        (
            jax.ShapeDtypeStruct((groups * 8, wide), BF16),
            jax.ShapeDtypeStruct((groups * 8, t), BF16),
            jax.ShapeDtypeStruct((groups * 8, t), BF16),
        ),
        scratch=[
            pltpu.VMEM((groups * 8, t), F32),
            pltpu.VMEM((pcols, t), F32),
            pltpu.VMEM((pcols, t), F32),
        ],
        inputs=3,
        name="grads",
    )(packs, proj, x)
    pieces = lax.all_to_all(contrib.reshape(groups, 8, wide), "fsdp", 0, 0)
    grad_inputs = call(
        back_kernel,
        jax.ShapeDtypeStruct((t, inner), BF16),
        inputs=4,
        name="back",
    )(main, tail, gathered, gx)
    total = pieces.astype(F32).sum(axis=0)
    wgrad = jnp.concatenate([total[:, :inner], total[:, inner:].reshape(2, inner)], axis=0)
    return (grad_inputs[None], wgrad.T[None])


def solution(mesh):
    placed = (
        P("pp", "fsdp", "tp"),
        P("pp", "fsdp", "tp"),
        P("pp", "tp", "fsdp"),
        P("pp", "tp"),
        P("pp", "tp"),
        P("pp", "tp"),
    )
    return jax.shard_map(
        per_device,
        mesh=mesh,
        in_specs=placed,
        out_specs=(P("pp", "fsdp", "tp"), P("pp", "tp", "fsdp")),
        check_vma=False,
    )
```

```python
import functools

import jax
import jax.numpy as jnp
from jax import lax
from jax.experimental import pallas as pl
from jax.experimental.pallas import tpu as pltpu
from jax.sharding import Mesh, PartitionSpec as P


HEAD_DIM = 64
STATE = 256
F32 = jnp.float32
BF16 = jnp.bfloat16
HIGHEST = lax.Precision.HIGHEST
NT = (((1,), (1,)), ((), ()))
NN = (((1,), (0,)), ((), ()))
VMEM_LIMIT = 20 * 1024 * 1024


def dot(a, b, dims=NN, precision=None):
    return lax.dot_general(a, b, dims, precision=precision, preferred_element_type=F32)


def call(kernel, outs, scratch=(), smem=(), inputs=0):
    specs = [
        pl.BlockSpec(memory_space=pltpu.SMEM if i in smem else pltpu.VMEM) for i in range(inputs)
    ]
    return pl.pallas_call(
        kernel,
        out_shape=outs,
        in_specs=specs,
        out_specs=jax.tree.map(lambda _: pl.BlockSpec(memory_space=pltpu.VMEM), outs),
        scratch_shapes=list(scratch),
        compiler_params=pltpu.CompilerParams(vmem_limit_bytes=VMEM_LIMIT),
    )


def natural(side, m, f):
    half = side // 2
    return 10 * ((2 * (f // half) + m // 2) * side + 2 * (f % half) + m % 2)


def project_kernel(w_ref, x0_ref, x1_ref, x2_ref, x3_ref, out_ref, tail_ref):
    far = w_ref.shape[0] // 8
    inner = x0_ref.shape[1]
    quarter = inner // 4
    for r, x_ref in enumerate((x0_ref, x1_ref, x2_ref, x3_ref)):
        out_ref[r, : 8 * far, :] = dot(w_ref[:, :inner], x_ref[...], NT)
        tail = None
        for q in range(4):
            tail_ref[r, q] = dot(w_ref[:, inner:], x_ref[:, q * quarter : (q + 1) * quarter], NT)
            part = tail_ref[r, q, pl.ds(q, 2 * far, 4), :]
            tail = part if tail is None else tail + part
        out_ref[r, 8 * far :, :] = tail


def as_column(row):
    n = row.shape[1]
    at = lax.broadcasted_iota(jnp.int32, (n, n), 0) == lax.broadcasted_iota(jnp.int32, (n, n), 1)
    return jnp.sum(jnp.where(at, jnp.broadcast_to(row, (n, n)), 0.0), axis=1, keepdims=True)


def prepare_kernel(rate_ref, bias_ref, out_ref):
    _, heads, t = out_ref.shape
    out_ref[0] = jnp.broadcast_to(as_column(jnp.exp(rate_ref[...])), (heads, t))
    out_ref[1] = jnp.broadcast_to(as_column(bias_ref[...]), (heads, t))


def core_kernel(
    side, tp_ref, gain_ref, group_ref, head_ref, g_ref, x_ref,
    pack_ref, gx_ref, proj_ref,
    cum_ref, cols_ref, row_ref, col_ref, scores_ref,
):
    heads = head_ref.shape[1]
    t = g_ref.shape[0]
    near, rows, _ = group_ref.shape
    far = rows // 10
    for m in range(near):
        for f in range(far):
            at = natural(side, m, f)
            proj_ref[at : at + 8, :] = group_ref[m, 8 * f : 8 * f + 8, :]
            last = 8 * far + 2 * f
            proj_ref[at + 8 : at + 10, :] = group_ref[m, last : last + 2, :]
    raw = proj_ref[pl.ds(pl.multiple_of(2 * STATE + tp_ref[0] * heads, heads), heads), :]
    z = raw + head_ref[1]
    rate = head_ref[0]
    step = jnp.maximum(z, 0.0) + jnp.log1p(jnp.exp(-jnp.abs(z)))
    first = lax.broadcasted_iota(jnp.int32, (t, t), 0)
    second = lax.broadcasted_iota(jnp.int32, (t, t), 1)
    cum = dot(-step * rate, jnp.where(first <= second, 1.0, 0.0), NN, HIGHEST)
    cum_ref[...] = cum
    cols_ref[...] = jnp.transpose(
        jnp.concatenate([cum, step, jnp.zeros((t - 2 * heads, t), F32)], axis=0)
    )
    scores = dot(jnp.transpose(proj_ref[:STATE, :]), proj_ref[STATE : 2 * STATE, :], NN, HIGHEST)
    causal = first <= second
    scores_ref[...] = jnp.where(causal, scores, 0.0)
    pack_ref[:t, :] = jnp.zeros((t, t), F32)
    left = second < HEAD_DIM

    def pair(k, carry):
        lanes = pl.ds(pl.multiple_of(k * 2 * HEAD_DIM, 2 * HEAD_DIM), 2 * HEAD_DIM)
        g = g_ref[:, lanes]
        x = x_ref[:, lanes]
        cols = cols_ref[...]
        none = jnp.zeros_like(g)
        gs = (jnp.where(left, g, none), jnp.where(left, none, g))
        moved = jnp.zeros((t, 2 * HEAD_DIM), F32)
        for a in range(2):
            h = 2 * k + a
            product = dot(x, gs[a], NT)
            step_col = cols[:, heads + a : heads + a + 1]
            decay = jnp.exp(jnp.minimum(cum_ref[pl.ds(h, 1), :] - cols[:, a : a + 1], 0.0))
            faded = product * decay
            stepped = faded * step_col
            pack_ref[:t, :] += stepped
            col_ref[...] = jnp.where(
                second == h,
                jnp.sum(faded * scores_ref[...], axis=1, keepdims=True),
                col_ref[...],
            )
            row_ref[pl.ds(h, 1), :] = jnp.sum(stepped * scores_ref[...], axis=0, keepdims=True)
            moved += dot((decay * scores_ref[...]).astype(BF16), gs[a], NN)
        step_both = jnp.where(left, cols[:, heads : heads + 1], cols[:, heads + 1 : heads + 2])
        gain = jnp.where(left, gain_ref[0, 2 * k], gain_ref[0, 2 * k + 1])
        up = g.astype(F32)
        gx_ref[:, lanes] = up + (moved * step_both + gain * up)
        cols_ref[...] = pltpu.roll(cols, t - 2, 1)
        return carry

    lax.fori_loop(0, heads // 2, pair, 0)
    pack_ref[:t, :] = jnp.where(causal, pack_ref[:t, :], 0.0)
    col = jnp.transpose(col_ref[...])[:heads, :]
    dcum = row_ref[...] - step * col
    decayed = dot(dcum, jnp.where(first >= second, 1.0, 0.0), NN, HIGHEST)
    pack_ref[t:, :] = (col - rate * decayed) * (1.0 / (1.0 + jnp.exp(-z)))


def grads_kernel(side, pack_ref, proj_ref, send_ref, grad_ref, rows_ref):
    parts, rows, t = pack_ref.shape
    heads = rows - t
    scores = pack_ref[0, :t, :]
    for p in range(1, parts):
        scores = scores + pack_ref[p, :t, :]
    grad_ref[:STATE, :] = dot(proj_ref[STATE : 2 * STATE, :], scores, NT, HIGHEST)
    grad_ref[STATE : 2 * STATE, :] = dot(proj_ref[:STATE, :], scores, NN, HIGHEST)
    for p in range(parts):
        grad_ref[2 * STATE + p * heads : 2 * STATE + (p + 1) * heads, :] = pack_ref[p, t:, :]
    near, rows, _ = send_ref.shape
    far = rows // 10
    for m in range(near):
        for f in range(far):
            at = natural(side, m, f)
            rows_ref[m, 8 * f : 8 * f + 8, :] = grad_ref[at : at + 8, :]
            last = 8 * far + 2 * f
            rows_ref[m, last : last + 2, :] = grad_ref[at + 8 : at + 10, :]
    send_ref[...] = rows_ref[...].astype(BF16)


def weight_kernel(who_ref, grad_ref, x0_ref, x1_ref, x2_ref, x3_ref, out_ref, wide_ref):
    far = grad_ref.shape[1] // 10
    inner = x0_ref.shape[1]
    quarter = inner // 4
    main = tail = 0.0
    for r, x_ref in enumerate((x0_ref, x1_ref, x2_ref, x3_ref)):
        grad = grad_ref[who_ref[r]]
        main = main + dot(grad[: 8 * far, :], x_ref[...])
        for q in range(4):
            wide_ref[r, pl.ds(q, 2 * far, 4), :] = grad[8 * far :, :].astype(F32)
        wide = wide_ref[r]
        quarter_of = lax.broadcasted_iota(jnp.int32, wide.shape, 0) % 4
        for q in range(4):
            piece = jnp.where(quarter_of == q, wide, 0.0).astype(BF16)
            tail = tail + dot(piece, x_ref[:, q * quarter : (q + 1) * quarter])
    out_ref[:, :inner] = main.astype(BF16)
    out_ref[:, inner:] = tail.astype(BF16)


def back_kernel(who_ref, grad_ref, w0_ref, w1_ref, w2_ref, w3_ref, gx_ref, out_ref, wide_ref):
    far = grad_ref.shape[1] // 10
    inner = gx_ref.shape[1]
    quarter = inner // 4
    w_refs = (w0_ref, w1_ref, w2_ref, w3_ref)
    mains, tails = [], []
    for r in range(4):
        grad = grad_ref[who_ref[r]].astype(F32)
        mains.append(jnp.transpose(grad[: 8 * far, :]).astype(BF16))
        for q in range(4):
            wide_ref[r, pl.ds(q, 2 * far, 4), :] = grad[8 * far :, :]
        tails.append(jnp.transpose(wide_ref[r]))
    quarter_of = lax.broadcasted_iota(jnp.int32, tails[0].shape, 1) % 4
    for q in range(4):
        lanes = slice(q * quarter, (q + 1) * quarter)
        back = 0.0
        for r in range(4):
            piece = jnp.where(quarter_of == q, tails[r], 0.0).astype(BF16)
            back = back + (dot(mains[r], w_refs[r][:, lanes]) + dot(piece, w_refs[r][:, inner:]))
        out_ref[:, lanes] = (gx_ref[:, lanes] + back).astype(BF16)


NEAR = ("xl", "zl")
FAR = ("xh", "zh")
ROWS = ("xh", "xl", "zh", "zl")


def from_near(value):
    count = lax.axis_size(NEAR)
    return [value] + [
        lax.ppermute(value, NEAR, [(m, m ^ r) for m in range(count)]) for r in range(1, count)
    ]


def per_device(saved_inputs, returned, proj_weight, log_rate, step_bias, skip_gain):
    x = saved_inputs[0]
    t, inner = x.shape
    heads = log_rate.shape[1]
    sections = lax.axis_size("pp")
    near = lax.axis_size(NEAR)
    far = lax.axis_size(FAR)
    side = lax.axis_size(("xh", "xl"))
    tps = lax.axis_size("tp")
    pcols = proj_weight.shape[2] * near * far
    rows = pcols // near
    wide = inner + 2 * inner // 8
    who = lax.axis_index(NEAR) ^ jnp.arange(near, dtype=jnp.int32)
    xs = from_near(x)
    arrived = lax.ppermute(returned, "pp", [(i, (i - 1) % sections) for i in range(sections)])[0]
    of_heads = call(
        prepare_kernel, jax.ShapeDtypeStruct((2, heads, t), F32), inputs=2
    )(log_rate, step_bias)

    w = proj_weight[0].T
    shard = jnp.concatenate([w[:8], w[8:].reshape(8, inner // 4)], axis=1)
    weight = lax.all_to_all(
        jnp.broadcast_to(shard[None], (far, 8, wide)), FAR, 0, 0
    ).reshape(far * 8, wide)
    weights = from_near(weight)

    partial = call(
        project_kernel,
        jax.ShapeDtypeStruct((near, rows, t), F32),
        scratch=[pltpu.VMEM((near, 4, far * 8, t), F32)],
        inputs=5,
    )(weight, *xs)
    share = lax.all_to_all(partial, "tp", 0, 0).sum(axis=0)
    own = lax.ppermute(
        share,
        NEAR + ("tp",),
        [(m * tps + k, (m ^ k) * tps + m) for m in range(near) for k in range(tps)],
    )
    proj = lax.all_gather(own, "tp", axis=0)

    pack, gx, proj = call(
        functools.partial(core_kernel, side),
        (
            jax.ShapeDtypeStruct((t + heads, t), F32),
            jax.ShapeDtypeStruct((t, inner), F32),
            jax.ShapeDtypeStruct((pcols, t), F32),
        ),
        scratch=[
            pltpu.VMEM((heads, t), F32),
            pltpu.VMEM((t, t), F32),
            pltpu.VMEM((heads, t), F32),
            pltpu.VMEM((t, t), F32),
            pltpu.VMEM((t, t), F32),
        ],
        smem=(0, 1),
        inputs=6,
    )(lax.axis_index("tp").reshape(1), skip_gain, proj, of_heads, arrived, x)

    packs = lax.all_gather(pack, "tp", axis=0)
    send = call(
        functools.partial(grads_kernel, side),
        jax.ShapeDtypeStruct((near, rows, t), BF16),
        scratch=[pltpu.VMEM((pcols, t), F32), pltpu.VMEM((near, rows, t), F32)],
        inputs=2,
    )(packs, proj)
    grads = lax.all_to_all(send, NEAR, 0, 0)
    contrib = call(
        weight_kernel,
        jax.ShapeDtypeStruct((far * 8, wide), BF16),
        scratch=[pltpu.VMEM((near, far * 8, t), F32)],
        smem=(0,),
        inputs=6,
    )(who, grads, *xs)
    pieces = lax.all_to_all(contrib.reshape(far, 8, wide), FAR, 0, 0)
    grad_inputs = call(
        back_kernel,
        jax.ShapeDtypeStruct((t, inner), BF16),
        scratch=[pltpu.VMEM((near, far * 8, t), F32)],
        smem=(0,),
        inputs=7,
    )(who, send, *weights, gx)
    total = pieces.astype(F32).sum(axis=0)
    wgrad = jnp.concatenate([total[:, :inner], total[:, inner:].reshape(2, inner)], axis=0)
    return (grad_inputs[None], wgrad.T[None])


def solution(mesh):
    side = 8
    fine = Mesh(
        mesh.devices.reshape(mesh.shape["pp"], side // 2, 2, side // 2, 2, mesh.shape["tp"]),
        ("pp", "xh", "xl", "zh", "zl", "tp"),
    )
    rows = ROWS
    placed = (
        P("pp", rows, "tp"),
        P("pp", rows, "tp"),
        P("pp", "tp", rows),
        P("pp", "tp"),
        P("pp", "tp"),
        P("pp", "tp"),
    )
    return jax.shard_map(
        per_device,
        mesh=fine,
        in_specs=placed,
        out_specs=(P("pp", rows, "tp"), P("pp", "tp", rows)),
        check_vma=False,
    )
```

```python
import functools

import jax
import jax.numpy as jnp
from jax import lax
from jax.experimental import pallas as pl
from jax.experimental.pallas import tpu as pltpu
from jax.sharding import Mesh, PartitionSpec as P


HEAD_DIM = 64
STATE = 256
F32 = jnp.float32
BF16 = jnp.bfloat16
HIGHEST = lax.Precision.HIGHEST
NT = (((1,), (1,)), ((), ()))
NN = (((1,), (0,)), ((), ()))
VMEM_LIMIT = 8 * 1024 * 1024


def dot(a, b, dims=NN, precision=None):
    return lax.dot_general(a, b, dims, precision=precision, preferred_element_type=F32)


def call(kernel, outs, scratch=(), smem=(), inputs=0):
    specs = [
        pl.BlockSpec(memory_space=pltpu.SMEM if i in smem else pltpu.VMEM) for i in range(inputs)
    ]
    return pl.pallas_call(
        kernel,
        out_shape=outs,
        in_specs=specs,
        out_specs=jax.tree.map(lambda _: pl.BlockSpec(memory_space=pltpu.VMEM), outs),
        scratch_shapes=list(scratch),
        compiler_params=pltpu.CompilerParams(vmem_limit_bytes=VMEM_LIMIT),
    )


def natural(side, m, f):
    half = side // 2
    return 10 * ((2 * (f // half) + m // 2) * side + 2 * (f % half) + m % 2)


def lanes_of(parts, start, count):
    width = parts[0].shape[1]
    at = start % width
    return parts[start // width][:, at : at + count]


def project_kernel(w_ref, x0_ref, x1_ref, x2_ref, xa_ref, xb_ref, out_ref, tail_ref):
    far = w_ref.shape[0] // 8
    inner = x0_ref.shape[1]
    quarter = inner // 4
    for r, parts in enumerate(((x0_ref,), (x1_ref,), (x2_ref,), (xa_ref, xb_ref))):
        width = inner // len(parts)
        main = 0.0
        for i, part in enumerate(parts):
            main = main + dot(w_ref[:, i * width : (i + 1) * width], part[...], NT)
        out_ref[r, : 8 * far, :] = main
        tail = 0.0
        for q in range(4):
            tail_ref[r, q] = dot(w_ref[:, inner:], lanes_of(parts, q * quarter, quarter), NT)
            tail = tail + tail_ref[r, q, pl.ds(q, 2 * far, 4), :]
        out_ref[r, 8 * far :, :] = tail


def as_column(row):
    n = row.shape[1]
    at = lax.broadcasted_iota(jnp.int32, (n, n), 0) == lax.broadcasted_iota(jnp.int32, (n, n), 1)
    return jnp.sum(jnp.where(at, jnp.broadcast_to(row, (n, n)), 0.0), axis=1, keepdims=True)


def bias_kernel(bias_ref, out_ref):
    out_ref[...] = jnp.broadcast_to(as_column(bias_ref[...]), out_ref.shape)


def rate_kernel(rate_ref, out_ref):
    out_ref[...] = jnp.broadcast_to(as_column(jnp.exp(rate_ref[...])), out_ref.shape)


def core_kernel(
    side, tp_ref, gain_ref, group_ref, rate_ref, bias_ref, g_ref, x_ref,
    pack_ref, gx_ref, proj_ref,
    cum_ref, cols_ref, row_ref, col_ref, scores_ref,
):
    heads = rate_ref.shape[0]
    t = g_ref.shape[0]
    near, rows, _ = group_ref.shape
    far = rows // 10
    for m in range(near):
        for f in range(far):
            at = natural(side, m, f)
            proj_ref[at : at + 8, :] = group_ref[m, 8 * f : 8 * f + 8, :]
            last = 8 * far + 2 * f
            proj_ref[at + 8 : at + 10, :] = group_ref[m, last : last + 2, :]
    raw = proj_ref[pl.ds(pl.multiple_of(2 * STATE + tp_ref[0] * heads, heads), heads), :]
    z = raw + bias_ref[...]
    rate = rate_ref[...]
    step = jnp.maximum(z, 0.0) + jnp.log1p(jnp.exp(-jnp.abs(z)))
    first = lax.broadcasted_iota(jnp.int32, (t, t), 0)
    second = lax.broadcasted_iota(jnp.int32, (t, t), 1)
    cum = dot(-step * rate, jnp.where(first <= second, 1.0, 0.0), NN, HIGHEST)
    cum_ref[...] = cum
    cols_ref[...] = jnp.transpose(
        jnp.concatenate([cum, step, jnp.zeros((t - 2 * heads, t), F32)], axis=0)
    )
    scores = dot(jnp.transpose(proj_ref[:STATE, :]), proj_ref[STATE : 2 * STATE, :], NN, HIGHEST)
    causal = first <= second
    scores_ref[...] = jnp.where(causal, scores, 0.0)
    pack_ref[:t, :] = jnp.zeros((t, t), F32)
    left = second < HEAD_DIM

    def pair(k, carry):
        lanes = pl.ds(pl.multiple_of(k * 2 * HEAD_DIM, 2 * HEAD_DIM), 2 * HEAD_DIM)
        g = g_ref[:, lanes]
        x = x_ref[:, lanes]
        cols = cols_ref[...]
        none = jnp.zeros_like(g)
        gs = (jnp.where(left, g, none), jnp.where(left, none, g))
        moved = jnp.zeros((t, 2 * HEAD_DIM), F32)
        for a in range(2):
            h = 2 * k + a
            product = dot(x, gs[a], NT)
            step_col = cols[:, heads + a : heads + a + 1]
            decay = jnp.exp(jnp.minimum(cum_ref[pl.ds(h, 1), :] - cols[:, a : a + 1], 0.0))
            faded = product * decay
            stepped = faded * step_col
            pack_ref[:t, :] += stepped
            col_ref[...] = jnp.where(
                second == h,
                jnp.sum(faded * scores_ref[...], axis=1, keepdims=True),
                col_ref[...],
            )
            row_ref[pl.ds(h, 1), :] = jnp.sum(stepped * scores_ref[...], axis=0, keepdims=True)
            moved += dot((decay * scores_ref[...]).astype(BF16), gs[a], NN)
        step_both = jnp.where(left, cols[:, heads : heads + 1], cols[:, heads + 1 : heads + 2])
        gain = jnp.where(left, gain_ref[0, 2 * k], gain_ref[0, 2 * k + 1])
        up = g.astype(F32)
        gx_ref[:, lanes] = up + (moved * step_both + gain * up)
        cols_ref[...] = pltpu.roll(cols, t - 2, 1)
        return carry

    lax.fori_loop(0, heads // 2, pair, 0)
    pack_ref[:t, :] = jnp.where(causal, pack_ref[:t, :], 0.0)
    col = jnp.transpose(col_ref[...])[:heads, :]
    dcum = row_ref[...] - step * col
    decayed = dot(dcum, jnp.where(first >= second, 1.0, 0.0), NN, HIGHEST)
    pack_ref[t:, :] = (col - rate * decayed) * (1.0 / (1.0 + jnp.exp(-z)))


def grads_kernel(side, pack_ref, proj_ref, send_ref, grad_ref, rows_ref):
    parts, rows, t = pack_ref.shape
    heads = rows - t
    scores = pack_ref[0, :t, :]
    for p in range(1, parts):
        scores = scores + pack_ref[p, :t, :]
    grad_ref[:STATE, :] = dot(proj_ref[STATE : 2 * STATE, :], scores, NT, HIGHEST)
    grad_ref[STATE : 2 * STATE, :] = dot(proj_ref[:STATE, :], scores, NN, HIGHEST)
    for p in range(parts):
        grad_ref[2 * STATE + p * heads : 2 * STATE + (p + 1) * heads, :] = pack_ref[p, t:, :]
    near, rows, _ = send_ref.shape
    far = rows // 10
    for m in range(near):
        for f in range(far):
            at = natural(side, m, f)
            rows_ref[m, 8 * f : 8 * f + 8, :] = grad_ref[at : at + 8, :]
            last = 8 * far + 2 * f
            rows_ref[m, last : last + 2, :] = grad_ref[at + 8 : at + 10, :]
    send_ref[...] = rows_ref[...].astype(BF16)


def weight_kernel(who_ref, grad_ref, x0_ref, x1_ref, x2_ref, xa_ref, xb_ref, out_ref, wide_ref):
    far = grad_ref.shape[1] // 10
    inner = x0_ref.shape[1]
    quarter = inner // 4
    half = inner // 2
    mains = [0.0, 0.0]
    tail = 0.0
    for r, parts in enumerate(((x0_ref,), (x1_ref,), (x2_ref,), (xa_ref, xb_ref))):
        grad = grad_ref[who_ref[r]]
        for i in range(2):
            mains[i] = mains[i] + dot(grad[: 8 * far, :], lanes_of(parts, i * half, half))
        for q in range(4):
            wide_ref[r, pl.ds(q, 2 * far, 4), :] = grad[8 * far :, :].astype(F32)
        wide = wide_ref[r]
        quarter_of = lax.broadcasted_iota(jnp.int32, wide.shape, 0) % 4
        for q in range(4):
            piece = jnp.where(quarter_of == q, wide, 0.0).astype(BF16)
            tail = tail + dot(piece, lanes_of(parts, q * quarter, quarter))
    out_ref[:, :half] = mains[0].astype(BF16)
    out_ref[:, half:inner] = mains[1].astype(BF16)
    out_ref[:, inner:] = tail.astype(BF16)


def back_kernel(who_ref, grad_ref, w0_ref, w1_ref, w2_ref, w3_ref, gx_ref, out_ref, wide_ref):
    far = grad_ref.shape[1] // 10
    inner = gx_ref.shape[1]
    quarter = inner // 4
    w_refs = (w0_ref, w1_ref, w2_ref, w3_ref)
    mains, tails = [], []
    for r in range(4):
        grad = grad_ref[who_ref[r]].astype(F32)
        mains.append(jnp.transpose(grad[: 8 * far, :]).astype(BF16))
        for q in range(4):
            wide_ref[r, pl.ds(q, 2 * far, 4), :] = grad[8 * far :, :]
        tails.append(jnp.transpose(wide_ref[r]))
    quarter_of = lax.broadcasted_iota(jnp.int32, tails[0].shape, 1) % 4
    for q in range(4):
        lanes = slice(q * quarter, (q + 1) * quarter)
        back = 0.0
        for r in range(4):
            piece = jnp.where(quarter_of == q, tails[r], 0.0).astype(BF16)
            back = back + (dot(mains[r], w_refs[r][:, lanes]) + dot(piece, w_refs[r][:, inner:]))
        out_ref[:, lanes] = (gx_ref[:, lanes] + back).astype(BF16)


NEAR = ("xl", "zl")
FAR = ("xh", "zh")
ROWS = ("xh", "xl", "zh", "zl")


def from_near(value, r):
    return lax.ppermute(value, NEAR, [(m, m ^ r) for m in range(lax.axis_size(NEAR))])


def per_device(saved_inputs, returned, proj_weight, log_rate, step_bias, skip_gain):
    x = saved_inputs[0]
    t, inner = x.shape
    heads = log_rate.shape[1]
    sections = lax.axis_size("pp")
    near = lax.axis_size(NEAR)
    far = lax.axis_size(FAR)
    side = lax.axis_size(("xh", "xl"))
    tps = lax.axis_size("tp")
    pcols = proj_weight.shape[2] * near * far
    rows = pcols // near
    wide = inner + 2 * inner // 8
    who = lax.axis_index(NEAR) ^ jnp.arange(near, dtype=jnp.int32)
    along_z, along_x = from_near(x, 1), from_near(x, 2)
    xs = [
        x,
        along_z,
        along_x,
        from_near(along_z[:, : inner // 2], 2),
        from_near(along_x[:, inner // 2 :], 1),
    ]
    arrived = lax.ppermute(returned, "pp", [(i, (i - 1) % sections) for i in range(sections)])[0]
    rates = call(rate_kernel, jax.ShapeDtypeStruct((heads, t), F32), inputs=1)(log_rate)
    biases = call(bias_kernel, jax.ShapeDtypeStruct((heads, t), F32), inputs=1)(step_bias)

    w = proj_weight[0].T
    shard = jnp.concatenate([w[:8], w[8:].reshape(8, inner // 4)], axis=1)
    weight = lax.all_to_all(
        jnp.broadcast_to(shard[None], (far, 8, wide)), FAR, 0, 0
    ).reshape(far * 8, wide)
    weights = [weight, from_near(weight, 1), from_near(weight, 2)]
    weights.append(from_near(weight, 3))

    partial = call(
        project_kernel,
        jax.ShapeDtypeStruct((near, rows, t), F32),
        scratch=[pltpu.VMEM((near, 4, far * 8, t), F32)],
        inputs=6,
    )(weight, *xs)
    share = lax.all_to_all(partial, "tp", 0, 0).sum(axis=0)
    own = lax.ppermute(
        share,
        NEAR + ("tp",),
        [(m * tps + k, (m ^ k) * tps + m) for m in range(near) for k in range(tps)],
    )
    proj = lax.all_gather(own, "tp", axis=0)

    pack, gx, proj = call(
        functools.partial(core_kernel, side),
        (
            jax.ShapeDtypeStruct((t + heads, t), F32),
            jax.ShapeDtypeStruct((t, inner), F32),
            jax.ShapeDtypeStruct((pcols, t), F32),
        ),
        scratch=[
            pltpu.VMEM((heads, t), F32),
            pltpu.VMEM((t, t), F32),
            pltpu.VMEM((heads, t), F32),
            pltpu.VMEM((t, t), F32),
            pltpu.VMEM((t, t), F32),
        ],
        smem=(0, 1),
        inputs=7,
    )(lax.axis_index("tp").reshape(1), skip_gain, proj, rates, biases, arrived, x)

    packs = lax.all_gather(pack, "tp", axis=0)
    send = call(
        functools.partial(grads_kernel, side),
        jax.ShapeDtypeStruct((near, rows, t), BF16),
        scratch=[pltpu.VMEM((pcols, t), F32), pltpu.VMEM((near, rows, t), F32)],
        inputs=2,
    )(packs, proj)
    grads = lax.all_to_all(send, NEAR, 0, 0)
    contrib = call(
        weight_kernel,
        jax.ShapeDtypeStruct((far * 8, wide), BF16),
        scratch=[pltpu.VMEM((near, far * 8, t), F32)],
        smem=(0,),
        inputs=7,
    )(who, grads, *xs)
    pieces = lax.all_to_all(contrib.reshape(far, 8, wide), FAR, 0, 0)
    grad_inputs = call(
        back_kernel,
        jax.ShapeDtypeStruct((t, inner), BF16),
        scratch=[pltpu.VMEM((near, far * 8, t), F32)],
        smem=(0,),
        inputs=7,
    )(who, send, *weights, gx)
    total = pieces.astype(F32).sum(axis=0)
    wgrad = jnp.concatenate([total[:, :inner], total[:, inner:].reshape(2, inner)], axis=0)
    return (grad_inputs[None], wgrad.T[None])


def solution(mesh):
    side = 8
    fine = Mesh(
        mesh.devices.reshape(mesh.shape["pp"], side // 2, 2, side // 2, 2, mesh.shape["tp"]),
        ("pp", "xh", "xl", "zh", "zl", "tp"),
    )
    rows = ROWS
    placed = (
        P("pp", rows, "tp"),
        P("pp", rows, "tp"),
        P("pp", "tp", rows),
        P("pp", "tp"),
        P("pp", "tp"),
        P("pp", "tp"),
    )
    return jax.shard_map(
        per_device,
        mesh=fine,
        in_specs=placed,
        out_specs=(P("pp", rows, "tp"), P("pp", "tp", rows)),
        check_vma=False,
    )
```

```python
import functools

import jax
import jax.numpy as jnp
from jax import lax
from jax.experimental import pallas as pl
from jax.experimental.pallas import tpu as pltpu
from jax.sharding import Mesh, PartitionSpec as P


HEAD_DIM = 64
STATE = 256
F32 = jnp.float32
BF16 = jnp.bfloat16
HIGHEST = lax.Precision.HIGHEST
NT = (((1,), (1,)), ((), ()))
NN = (((1,), (0,)), ((), ()))
VMEM_LIMIT = 8 * 1024 * 1024


def dot(a, b, dims=NN, precision=None):
    return lax.dot_general(a, b, dims, precision=precision, preferred_element_type=F32)


def call(kernel, outs, scratch=(), smem=(), inputs=0):
    specs = [
        pl.BlockSpec(memory_space=pltpu.SMEM if i in smem else pltpu.VMEM) for i in range(inputs)
    ]
    return pl.pallas_call(
        kernel,
        out_shape=outs,
        in_specs=specs,
        out_specs=jax.tree.map(lambda _: pl.BlockSpec(memory_space=pltpu.VMEM), outs),
        scratch_shapes=list(scratch),
        compiler_params=pltpu.CompilerParams(vmem_limit_bytes=VMEM_LIMIT),
    )


def natural(side, m, f):
    half = side // 2
    return 10 * ((2 * (f // half) + m // 2) * side + 2 * (f % half) + m % 2)


def project_kernel(w_ref, x0_ref, x1_ref, x2_ref, x3_ref, out_ref, tail_ref):
    far = w_ref.shape[0] // 8
    inner = x0_ref.shape[1]
    quarter = inner // 4
    for r, x_ref in enumerate((x0_ref, x1_ref, x2_ref, x3_ref)):
        out_ref[r, : 8 * far, :] = dot(w_ref[:, :inner], x_ref[...], NT)
        tail = None
        for q in range(4):
            tail_ref[r, q] = dot(w_ref[:, inner:], x_ref[:, q * quarter : (q + 1) * quarter], NT)
            part = tail_ref[r, q, pl.ds(q, 2 * far, 4), :]
            tail = part if tail is None else tail + part
        out_ref[r, 8 * far :, :] = tail


def as_column(row):
    n = row.shape[1]
    at = lax.broadcasted_iota(jnp.int32, (n, n), 0) == lax.broadcasted_iota(jnp.int32, (n, n), 1)
    return jnp.sum(jnp.where(at, jnp.broadcast_to(row, (n, n)), 0.0), axis=1, keepdims=True)


def bias_kernel(bias_ref, out_ref):
    out_ref[...] = jnp.broadcast_to(as_column(bias_ref[...]), out_ref.shape)


def rate_kernel(rate_ref, out_ref):
    out_ref[...] = jnp.broadcast_to(as_column(jnp.exp(rate_ref[...])), out_ref.shape)


def core_kernel(
    side, tp_ref, gain_ref, group_ref, rate_ref, bias_ref, g_ref, x_ref,
    pack_ref, gx_ref, proj_ref,
    cum_ref, cols_ref, row_ref, col_ref, scores_ref,
):
    heads = rate_ref.shape[0]
    t = g_ref.shape[0]
    near, rows, _ = group_ref.shape
    far = rows // 10
    for m in range(near):
        for f in range(far):
            at = natural(side, m, f)
            proj_ref[at : at + 8, :] = group_ref[m, 8 * f : 8 * f + 8, :]
            last = 8 * far + 2 * f
            proj_ref[at + 8 : at + 10, :] = group_ref[m, last : last + 2, :]
    raw = proj_ref[pl.ds(pl.multiple_of(2 * STATE + tp_ref[0] * heads, heads), heads), :]
    z = raw + bias_ref[...]
    rate = rate_ref[...]
    step = jnp.maximum(z, 0.0) + jnp.log1p(jnp.exp(-jnp.abs(z)))
    first = lax.broadcasted_iota(jnp.int32, (t, t), 0)
    second = lax.broadcasted_iota(jnp.int32, (t, t), 1)
    cum = dot(-step * rate, jnp.where(first <= second, 1.0, 0.0), NN, HIGHEST)
    cum_ref[...] = cum
    cols_ref[...] = jnp.transpose(
        jnp.concatenate([cum, step, jnp.zeros((t - 2 * heads, t), F32)], axis=0)
    )
    scores = dot(jnp.transpose(proj_ref[:STATE, :]), proj_ref[STATE : 2 * STATE, :], NN, HIGHEST)
    causal = first <= second
    scores_ref[...] = jnp.where(causal, scores, 0.0)
    pack_ref[:t, :] = jnp.zeros((t, t), F32)
    left = second < HEAD_DIM

    def pair(k, carry):
        lanes = pl.ds(pl.multiple_of(k * 2 * HEAD_DIM, 2 * HEAD_DIM), 2 * HEAD_DIM)
        g = g_ref[:, lanes]
        x = x_ref[:, lanes]
        cols = cols_ref[...]
        none = jnp.zeros_like(g)
        gs = (jnp.where(left, g, none), jnp.where(left, none, g))
        moved = jnp.zeros((t, 2 * HEAD_DIM), F32)
        for a in range(2):
            h = 2 * k + a
            product = dot(x, gs[a], NT)
            step_col = cols[:, heads + a : heads + a + 1]
            decay = jnp.exp(jnp.minimum(cum_ref[pl.ds(h, 1), :] - cols[:, a : a + 1], 0.0))
            faded = product * decay
            stepped = faded * step_col
            pack_ref[:t, :] += stepped
            col_ref[...] = jnp.where(
                second == h,
                jnp.sum(faded * scores_ref[...], axis=1, keepdims=True),
                col_ref[...],
            )
            row_ref[pl.ds(h, 1), :] = jnp.sum(stepped * scores_ref[...], axis=0, keepdims=True)
            moved += dot((decay * scores_ref[...]).astype(BF16), gs[a], NN)
        step_both = jnp.where(left, cols[:, heads : heads + 1], cols[:, heads + 1 : heads + 2])
        gain = jnp.where(left, gain_ref[0, 2 * k], gain_ref[0, 2 * k + 1])
        up = g.astype(F32)
        gx_ref[:, lanes] = up + (moved * step_both + gain * up)
        cols_ref[...] = pltpu.roll(cols, t - 2, 1)
        return carry

    lax.fori_loop(0, heads // 2, pair, 0)
    pack_ref[:t, :] = jnp.where(causal, pack_ref[:t, :], 0.0)
    col = jnp.transpose(col_ref[...])[:heads, :]
    dcum = row_ref[...] - step * col
    decayed = dot(dcum, jnp.where(first >= second, 1.0, 0.0), NN, HIGHEST)
    pack_ref[t:, :] = (col - rate * decayed) * (1.0 / (1.0 + jnp.exp(-z)))


def grads_kernel(side, pack_ref, proj_ref, send_ref, grad_ref, rows_ref):
    parts, rows, t = pack_ref.shape
    heads = rows - t
    scores = pack_ref[0, :t, :]
    for p in range(1, parts):
        scores = scores + pack_ref[p, :t, :]
    grad_ref[:STATE, :] = dot(proj_ref[STATE : 2 * STATE, :], scores, NT, HIGHEST)
    grad_ref[STATE : 2 * STATE, :] = dot(proj_ref[:STATE, :], scores, NN, HIGHEST)
    for p in range(parts):
        grad_ref[2 * STATE + p * heads : 2 * STATE + (p + 1) * heads, :] = pack_ref[p, t:, :]
    near, rows, _ = send_ref.shape
    far = rows // 10
    for m in range(near):
        for f in range(far):
            at = natural(side, m, f)
            rows_ref[m, 8 * f : 8 * f + 8, :] = grad_ref[at : at + 8, :]
            last = 8 * far + 2 * f
            rows_ref[m, last : last + 2, :] = grad_ref[at + 8 : at + 10, :]
    send_ref[...] = rows_ref[...].astype(BF16)


def weight_kernel(who_ref, grad_ref, x0_ref, x1_ref, x2_ref, x3_ref, out_ref, wide_ref):
    far = grad_ref.shape[1] // 10
    inner = x0_ref.shape[1]
    quarter = inner // 4
    main = tail = 0.0
    for r, x_ref in enumerate((x0_ref, x1_ref, x2_ref, x3_ref)):
        grad = grad_ref[who_ref[r]]
        main = main + dot(grad[: 8 * far, :], x_ref[...])
        for q in range(4):
            wide_ref[r, pl.ds(q, 2 * far, 4), :] = grad[8 * far :, :].astype(F32)
        wide = wide_ref[r]
        quarter_of = lax.broadcasted_iota(jnp.int32, wide.shape, 0) % 4
        for q in range(4):
            piece = jnp.where(quarter_of == q, wide, 0.0).astype(BF16)
            tail = tail + dot(piece, x_ref[:, q * quarter : (q + 1) * quarter])
    out_ref[:, :inner] = main.astype(BF16)
    out_ref[:, inner:] = tail.astype(BF16)


def back_kernel(who_ref, grad_ref, w0_ref, w1_ref, w2_ref, w3_ref, gx_ref, out_ref, wide_ref):
    far = grad_ref.shape[1] // 10
    inner = gx_ref.shape[1]
    quarter = inner // 4
    w_refs = (w0_ref, w1_ref, w2_ref, w3_ref)
    mains, tails = [], []
    for r in range(4):
        grad = grad_ref[who_ref[r]].astype(F32)
        mains.append(jnp.transpose(grad[: 8 * far, :]).astype(BF16))
        for q in range(4):
            wide_ref[r, pl.ds(q, 2 * far, 4), :] = grad[8 * far :, :]
        tails.append(jnp.transpose(wide_ref[r]))
    quarter_of = lax.broadcasted_iota(jnp.int32, tails[0].shape, 1) % 4
    for q in range(4):
        lanes = slice(q * quarter, (q + 1) * quarter)
        back = 0.0
        for r in range(4):
            piece = jnp.where(quarter_of == q, tails[r], 0.0).astype(BF16)
            back = back + (dot(mains[r], w_refs[r][:, lanes]) + dot(piece, w_refs[r][:, inner:]))
        out_ref[:, lanes] = (gx_ref[:, lanes] + back).astype(BF16)


NEAR = ("xl", "zl")
FAR = ("xh", "zh")
ROWS = ("xh", "xl", "zh", "zl")


def from_near(value):
    count = lax.axis_size(NEAR)
    return [value] + [
        lax.ppermute(value, NEAR, [(m, m ^ r) for m in range(count)]) for r in range(1, count)
    ]


def per_device(saved_inputs, returned, proj_weight, log_rate, step_bias, skip_gain):
    x = saved_inputs[0]
    t, inner = x.shape
    heads = log_rate.shape[1]
    sections = lax.axis_size("pp")
    near = lax.axis_size(NEAR)
    far = lax.axis_size(FAR)
    side = lax.axis_size(("xh", "xl"))
    tps = lax.axis_size("tp")
    pcols = proj_weight.shape[2] * near * far
    rows = pcols // near
    wide = inner + 2 * inner // 8
    who = lax.axis_index(NEAR) ^ jnp.arange(near, dtype=jnp.int32)
    xs = from_near(x)
    arrived = lax.ppermute(returned, "pp", [(i, (i - 1) % sections) for i in range(sections)])[0]
    rates = call(rate_kernel, jax.ShapeDtypeStruct((heads, t), F32), inputs=1)(log_rate)
    biases = call(bias_kernel, jax.ShapeDtypeStruct((heads, t), F32), inputs=1)(step_bias)

    w = proj_weight[0].T
    shard = jnp.concatenate([w[:8], w[8:].reshape(8, inner // 4)], axis=1)
    weight = lax.all_to_all(
        jnp.broadcast_to(shard[None], (far, 8, wide)), FAR, 0, 0
    ).reshape(far * 8, wide)
    weights = from_near(weight)

    partial = call(
        project_kernel,
        jax.ShapeDtypeStruct((near, rows, t), F32),
        scratch=[pltpu.VMEM((near, 4, far * 8, t), F32)],
        inputs=5,
    )(weight, *xs)
    share = lax.all_to_all(partial, "tp", 0, 0).sum(axis=0)
    own = lax.ppermute(
        share,
        NEAR + ("tp",),
        [(m * tps + k, (m ^ k) * tps + m) for m in range(near) for k in range(tps)],
    )
    proj = lax.all_gather(own, "tp", axis=0)

    pack, gx, proj = call(
        functools.partial(core_kernel, side),
        (
            jax.ShapeDtypeStruct((t + heads, t), F32),
            jax.ShapeDtypeStruct((t, inner), F32),
            jax.ShapeDtypeStruct((pcols, t), F32),
        ),
        scratch=[
            pltpu.VMEM((heads, t), F32),
            pltpu.VMEM((t, t), F32),
            pltpu.VMEM((heads, t), F32),
            pltpu.VMEM((t, t), F32),
            pltpu.VMEM((t, t), F32),
        ],
        smem=(0, 1),
        inputs=7,
    )(lax.axis_index("tp").reshape(1), skip_gain, proj, rates, biases, arrived, x)

    packs = lax.all_gather(pack, "tp", axis=0)
    send = call(
        functools.partial(grads_kernel, side),
        jax.ShapeDtypeStruct((near, rows, t), BF16),
        scratch=[pltpu.VMEM((pcols, t), F32), pltpu.VMEM((near, rows, t), F32)],
        inputs=2,
    )(packs, proj)
    grads = lax.all_to_all(send, NEAR, 0, 0)
    contrib = call(
        weight_kernel,
        jax.ShapeDtypeStruct((far * 8, wide), BF16),
        scratch=[pltpu.VMEM((near, far * 8, t), F32)],
        smem=(0,),
        inputs=6,
    )(who, grads, *xs)
    pieces = lax.all_to_all(contrib.reshape(far, 8, wide), FAR, 0, 0)
    grad_inputs = call(
        back_kernel,
        jax.ShapeDtypeStruct((t, inner), BF16),
        scratch=[pltpu.VMEM((near, far * 8, t), F32)],
        smem=(0,),
        inputs=7,
    )(who, send, *weights, gx)
    total = pieces.astype(F32).sum(axis=0)
    wgrad = jnp.concatenate([total[:, :inner], total[:, inner:].reshape(2, inner)], axis=0)
    return (grad_inputs[None], wgrad.T[None])


def solution(mesh):
    side = 8
    fine = Mesh(
        mesh.devices.reshape(mesh.shape["pp"], side // 2, 2, side // 2, 2, mesh.shape["tp"]),
        ("pp", "xh", "xl", "zh", "zl", "tp"),
    )
    rows = ROWS
    placed = (
        P("pp", rows, "tp"),
        P("pp", rows, "tp"),
        P("pp", "tp", rows),
        P("pp", "tp"),
        P("pp", "tp"),
        P("pp", "tp"),
    )
    return jax.shard_map(
        per_device,
        mesh=fine,
        in_specs=placed,
        out_specs=(P("pp", rows, "tp"), P("pp", "tp", rows)),
        check_vma=False,
    )
```

```python
import functools

import jax
import jax.numpy as jnp
from jax import lax
from jax.experimental import pallas as pl
from jax.experimental.pallas import tpu as pltpu
from jax.sharding import Mesh, PartitionSpec as P


HEAD_DIM = 64
STATE = 256
F32 = jnp.float32
BF16 = jnp.bfloat16
HIGHEST = lax.Precision.HIGHEST
NT = (((1,), (1,)), ((), ()))
NN = (((1,), (0,)), ((), ()))
VMEM_LIMIT = 8 * 1024 * 1024


def dot(a, b, dims=NN, precision=None):
    return lax.dot_general(a, b, dims, precision=precision, preferred_element_type=F32)


def call(kernel, outs, scratch=(), smem=(), inputs=0):
    specs = [
        pl.BlockSpec(memory_space=pltpu.SMEM if i in smem else pltpu.VMEM) for i in range(inputs)
    ]
    return pl.pallas_call(
        kernel,
        out_shape=outs,
        in_specs=specs,
        out_specs=jax.tree.map(lambda _: pl.BlockSpec(memory_space=pltpu.VMEM), outs),
        scratch_shapes=list(scratch),
        compiler_params=pltpu.CompilerParams(vmem_limit_bytes=VMEM_LIMIT),
    )


def natural(side, m, f):
    half = side // 2
    return 10 * ((2 * (f // half) + m // 2) * side + 2 * (f % half) + m % 2)


def project_kernel(w_ref, x0_ref, x1_ref, x2_ref, x3_ref, out_ref, tail_ref):
    far = w_ref.shape[0] // 8
    inner = x0_ref.shape[1]
    quarter = inner // 4
    for r, x_ref in enumerate((x0_ref, x1_ref, x2_ref, x3_ref)):
        out_ref[r, : 8 * far, :] = dot(w_ref[:, :inner], x_ref[...], NT)
        tail = None
        for q in range(4):
            tail_ref[r, q] = dot(w_ref[:, inner:], x_ref[:, q * quarter : (q + 1) * quarter], NT)
            part = tail_ref[r, q, pl.ds(q, 2 * far, 4), :]
            tail = part if tail is None else tail + part
        out_ref[r, 8 * far :, :] = tail


def as_column(row):
    n = row.shape[1]
    at = lax.broadcasted_iota(jnp.int32, (n, n), 0) == lax.broadcasted_iota(jnp.int32, (n, n), 1)
    return jnp.sum(jnp.where(at, jnp.broadcast_to(row, (n, n)), 0.0), axis=1, keepdims=True)


def bias_kernel(bias_ref, out_ref):
    out_ref[...] = jnp.broadcast_to(as_column(bias_ref[...]), out_ref.shape)


def rate_kernel(rate_ref, out_ref):
    out_ref[...] = jnp.broadcast_to(as_column(jnp.exp(rate_ref[...])), out_ref.shape)


def core_kernel(
    side, tp_ref, gain_ref, group_ref, rate_ref, bias_ref, g_ref, x_ref,
    pack_ref, gx_ref, proj_ref,
    cum_ref, cols_ref, row_ref, col_ref, scores_ref,
):
    heads = rate_ref.shape[0]
    t = g_ref.shape[0]
    near, rows, _ = group_ref.shape
    far = rows // 10
    for m in range(near):
        for f in range(far):
            at = natural(side, m, f)
            proj_ref[at : at + 8, :] = group_ref[m, 8 * f : 8 * f + 8, :]
            last = 8 * far + 2 * f
            proj_ref[at + 8 : at + 10, :] = group_ref[m, last : last + 2, :]
    raw = proj_ref[pl.ds(pl.multiple_of(2 * STATE + tp_ref[0] * heads, heads), heads), :]
    z = raw + bias_ref[...]
    rate = rate_ref[...]
    step = jnp.maximum(z, 0.0) + jnp.log1p(jnp.exp(-jnp.abs(z)))
    first = lax.broadcasted_iota(jnp.int32, (t, t), 0)
    second = lax.broadcasted_iota(jnp.int32, (t, t), 1)
    cum = dot(-step * rate, jnp.where(first <= second, 1.0, 0.0), NN, HIGHEST)
    cum_ref[...] = cum
    cols_ref[...] = jnp.transpose(
        jnp.concatenate([cum, step, jnp.zeros((t - 2 * heads, t), F32)], axis=0)
    )
    scores = dot(jnp.transpose(proj_ref[:STATE, :]), proj_ref[STATE : 2 * STATE, :], NN, HIGHEST)
    causal = first <= second
    scores_ref[...] = jnp.where(causal, scores, 0.0)
    pack_ref[:t, :] = jnp.zeros((t, t), F32)
    left = second < HEAD_DIM

    def pair(k, carry):
        lanes = pl.ds(pl.multiple_of(k * 2 * HEAD_DIM, 2 * HEAD_DIM), 2 * HEAD_DIM)
        g = g_ref[:, lanes]
        x = x_ref[:, lanes]
        cols = cols_ref[...]
        none = jnp.zeros_like(g)
        gs = (jnp.where(left, g, none), jnp.where(left, none, g))
        moved = jnp.zeros((t, 2 * HEAD_DIM), F32)
        for a in range(2):
            h = 2 * k + a
            product = dot(x, gs[a], NT)
            step_col = cols[:, heads + a : heads + a + 1]
            decay = jnp.exp(jnp.minimum(cum_ref[pl.ds(h, 1), :] - cols[:, a : a + 1], 0.0))
            faded = product * decay
            stepped = faded * step_col
            pack_ref[:t, :] += stepped
            col_ref[...] = jnp.where(
                second == h,
                jnp.sum(faded * scores_ref[...], axis=1, keepdims=True),
                col_ref[...],
            )
            row_ref[pl.ds(h, 1), :] = jnp.sum(stepped * scores_ref[...], axis=0, keepdims=True)
            moved += dot((decay * scores_ref[...]).astype(BF16), gs[a], NN)
        step_both = jnp.where(left, cols[:, heads : heads + 1], cols[:, heads + 1 : heads + 2])
        gain = jnp.where(left, gain_ref[0, 2 * k], gain_ref[0, 2 * k + 1])
        up = g.astype(F32)
        gx_ref[:, lanes] = up + (moved * step_both + gain * up)
        cols_ref[...] = pltpu.roll(cols, t - 2, 1)
        return carry

    lax.fori_loop(0, heads // 2, pair, 0)
    pack_ref[:t, :] = jnp.where(causal, pack_ref[:t, :], 0.0)
    col = jnp.transpose(col_ref[...])[:heads, :]
    dcum = row_ref[...] - step * col
    decayed = dot(dcum, jnp.where(first >= second, 1.0, 0.0), NN, HIGHEST)
    pack_ref[t:, :] = (col - rate * decayed) * (1.0 / (1.0 + jnp.exp(-z)))


def grads_kernel(side, pack_ref, proj_ref, send_ref, grad_ref, rows_ref):
    parts, rows, t = pack_ref.shape
    heads = rows - t
    scores = pack_ref[0, :t, :]
    for p in range(1, parts):
        scores = scores + pack_ref[p, :t, :]
    grad_ref[:STATE, :] = dot(proj_ref[STATE : 2 * STATE, :], scores, NT, HIGHEST)
    grad_ref[STATE : 2 * STATE, :] = dot(proj_ref[:STATE, :], scores, NN, HIGHEST)
    for p in range(parts):
        grad_ref[2 * STATE + p * heads : 2 * STATE + (p + 1) * heads, :] = pack_ref[p, t:, :]
    near, rows, _ = send_ref.shape
    far = rows // 10
    for m in range(near):
        for f in range(far):
            at = natural(side, m, f)
            rows_ref[m, 8 * f : 8 * f + 8, :] = grad_ref[at : at + 8, :]
            last = 8 * far + 2 * f
            rows_ref[m, last : last + 2, :] = grad_ref[at + 8 : at + 10, :]
    send_ref[...] = rows_ref[...].astype(BF16)


def weight_kernel(who_ref, grad_ref, x0_ref, x1_ref, x2_ref, x3_ref, out_ref, wide_ref):
    far = grad_ref.shape[1] // 10
    inner = x0_ref.shape[1]
    quarter = inner // 4
    main = tail = 0.0
    for r, x_ref in enumerate((x0_ref, x1_ref, x2_ref, x3_ref)):
        grad = grad_ref[who_ref[r]]
        main = main + dot(grad[: 8 * far, :], x_ref[...])
        for q in range(4):
            wide_ref[r, pl.ds(q, 2 * far, 4), :] = grad[8 * far :, :].astype(F32)
        wide = wide_ref[r]
        quarter_of = lax.broadcasted_iota(jnp.int32, wide.shape, 0) % 4
        for q in range(4):
            piece = jnp.where(quarter_of == q, wide, 0.0).astype(BF16)
            tail = tail + dot(piece, x_ref[:, q * quarter : (q + 1) * quarter])
    out_ref[:, :inner] = main.astype(BF16)
    out_ref[:, inner:] = tail.astype(BF16)


def back_kernel(who_ref, grad_ref, w0_ref, w1_ref, w2_ref, w3_ref, gx_ref, out_ref, wide_ref):
    far = grad_ref.shape[1] // 10
    inner = gx_ref.shape[1]
    quarter = inner // 4
    w_refs = (w0_ref, w1_ref, w2_ref, w3_ref)
    mains, tails = [], []
    for r in range(4):
        grad = grad_ref[who_ref[r]].astype(F32)
        mains.append(jnp.transpose(grad[: 8 * far, :]).astype(BF16))
        for q in range(4):
            wide_ref[r, pl.ds(q, 2 * far, 4), :] = grad[8 * far :, :]
        tails.append(jnp.transpose(wide_ref[r]))
    quarter_of = lax.broadcasted_iota(jnp.int32, tails[0].shape, 1) % 4
    for q in range(4):
        lanes = slice(q * quarter, (q + 1) * quarter)
        back = 0.0
        for r in range(4):
            piece = jnp.where(quarter_of == q, tails[r], 0.0).astype(BF16)
            back = back + (dot(mains[r], w_refs[r][:, lanes]) + dot(piece, w_refs[r][:, inner:]))
        out_ref[:, lanes] = (gx_ref[:, lanes] + back).astype(BF16)


NEAR = ("xl", "zl")
FAR = ("xh", "zh")
ROWS = ("xh", "xl", "zh", "zl")


def from_near(value, r):
    return lax.ppermute(value, NEAR, [(m, m ^ r) for m in range(lax.axis_size(NEAR))])


def per_device(saved_inputs, returned, proj_weight, log_rate, step_bias, skip_gain):
    x = saved_inputs[0]
    t, inner = x.shape
    heads = log_rate.shape[1]
    sections = lax.axis_size("pp")
    near = lax.axis_size(NEAR)
    far = lax.axis_size(FAR)
    side = lax.axis_size(("xh", "xl"))
    tps = lax.axis_size("tp")
    pcols = proj_weight.shape[2] * near * far
    rows = pcols // near
    wide = inner + 2 * inner // 8
    who = lax.axis_index(NEAR) ^ jnp.arange(near, dtype=jnp.int32)
    xs = [x] + [from_near(x, r) for r in range(1, near)]
    arrived = lax.ppermute(returned, "pp", [(i, (i - 1) % sections) for i in range(sections)])[0]
    rates = call(rate_kernel, jax.ShapeDtypeStruct((heads, t), F32), inputs=1)(log_rate)
    biases = call(bias_kernel, jax.ShapeDtypeStruct((heads, t), F32), inputs=1)(step_bias)

    w = proj_weight[0].T
    shard = jnp.concatenate([w[:8], w[8:].reshape(8, inner // 4)], axis=1)
    weight = lax.all_to_all(
        jnp.broadcast_to(shard[None], (far, 8, wide)), FAR, 0, 0
    ).reshape(far * 8, wide)
    diagonal = from_near(weight, 3)
    weights = [weight, from_near(weight, 1), from_near(weight, 2), diagonal]

    partial = call(
        project_kernel,
        jax.ShapeDtypeStruct((near, rows, t), F32),
        scratch=[pltpu.VMEM((near, 4, far * 8, t), F32)],
        inputs=5,
    )(weight, *xs)
    share = lax.all_to_all(partial, "tp", 0, 0).sum(axis=0)
    own = lax.ppermute(
        share,
        NEAR + ("tp",),
        [(m * tps + k, (m ^ k) * tps + m) for m in range(near) for k in range(tps)],
    )
    proj = lax.all_gather(own, "tp", axis=0)

    pack, gx, proj = call(
        functools.partial(core_kernel, side),
        (
            jax.ShapeDtypeStruct((t + heads, t), F32),
            jax.ShapeDtypeStruct((t, inner), F32),
            jax.ShapeDtypeStruct((pcols, t), F32),
        ),
        scratch=[
            pltpu.VMEM((heads, t), F32),
            pltpu.VMEM((t, t), F32),
            pltpu.VMEM((heads, t), F32),
            pltpu.VMEM((t, t), F32),
            pltpu.VMEM((t, t), F32),
        ],
        smem=(0, 1),
        inputs=7,
    )(lax.axis_index("tp").reshape(1), skip_gain, proj, rates, biases, arrived, x)

    packs = lax.all_gather(pack, "tp", axis=0)
    send = call(
        functools.partial(grads_kernel, side),
        jax.ShapeDtypeStruct((near, rows, t), BF16),
        scratch=[pltpu.VMEM((pcols, t), F32), pltpu.VMEM((near, rows, t), F32)],
        inputs=2,
    )(packs, proj)
    grads = lax.all_to_all(send, NEAR, 0, 0)
    contrib = call(
        weight_kernel,
        jax.ShapeDtypeStruct((far * 8, wide), BF16),
        scratch=[pltpu.VMEM((near, far * 8, t), F32)],
        smem=(0,),
        inputs=6,
    )(who, grads, *xs)
    pieces = lax.all_to_all(contrib.reshape(far, 8, wide), FAR, 0, 0)
    grad_inputs = call(
        back_kernel,
        jax.ShapeDtypeStruct((t, inner), BF16),
        scratch=[pltpu.VMEM((near, far * 8, t), F32)],
        smem=(0,),
        inputs=7,
    )(who, send, *weights, gx)
    total = pieces.astype(F32).sum(axis=0)
    wgrad = jnp.concatenate([total[:, :inner], total[:, inner:].reshape(2, inner)], axis=0)
    return (grad_inputs[None], wgrad.T[None])


def solution(mesh):
    side = 8
    fine = Mesh(
        mesh.devices.reshape(mesh.shape["pp"], side // 2, 2, side // 2, 2, mesh.shape["tp"]),
        ("pp", "xh", "xl", "zh", "zl", "tp"),
    )
    rows = ROWS
    placed = (
        P("pp", rows, "tp"),
        P("pp", rows, "tp"),
        P("pp", "tp", rows),
        P("pp", "tp"),
        P("pp", "tp"),
        P("pp", "tp"),
    )
    return jax.shard_map(
        per_device,
        mesh=fine,
        in_specs=placed,
        out_specs=(P("pp", rows, "tp"), P("pp", "tp", rows)),
        check_vma=False,
    )
```

```python
import functools

import jax
import jax.numpy as jnp
from jax import lax
from jax.experimental import pallas as pl
from jax.experimental.pallas import tpu as pltpu
from jax.sharding import Mesh, PartitionSpec as P


HEAD_DIM = 64
STATE = 256
F32 = jnp.float32
BF16 = jnp.bfloat16
HIGHEST = lax.Precision.HIGHEST
NT = (((1,), (1,)), ((), ()))
NN = (((1,), (0,)), ((), ()))
VMEM_LIMIT = 8 * 1024 * 1024


def dot(a, b, dims=NN, precision=None):
    return lax.dot_general(a, b, dims, precision=precision, preferred_element_type=F32)


def call(kernel, outs, scratch=(), smem=(), inputs=0):
    specs = [
        pl.BlockSpec(memory_space=pltpu.SMEM if i in smem else pltpu.VMEM) for i in range(inputs)
    ]
    return pl.pallas_call(
        kernel,
        out_shape=outs,
        in_specs=specs,
        out_specs=jax.tree.map(lambda _: pl.BlockSpec(memory_space=pltpu.VMEM), outs),
        scratch_shapes=list(scratch),
        compiler_params=pltpu.CompilerParams(vmem_limit_bytes=VMEM_LIMIT),
    )


def natural(side, m, f):
    half = side // 2
    return 10 * ((2 * (f // half) + m // 2) * side + 2 * (f % half) + m % 2)


def shard_kernel(w_ref, out_ref, row_ref):
    copies, _, _ = out_ref.shape
    inner = w_ref.shape[1]
    quarter = inner // 4
    w = w_ref[...].astype(F32)
    row_ref[:, :inner] = w[:8, :]
    for c in range(2):
        for q in range(4):
            row_ref[4 * c + q : 4 * c + q + 1, inner:] = w[
                8 + c : 9 + c, q * quarter : (q + 1) * quarter
            ]
    row = row_ref[...].astype(BF16)
    for i in range(copies):
        out_ref[i] = row


def total_kernel(piece_ref, out_ref):
    count, _, wide = piece_ref.shape
    blocks = wide // 160
    inner = blocks * 128
    total = piece_ref[0].astype(F32)
    for i in range(1, count):
        total = total + piece_ref[i].astype(F32)
    for b in range(blocks):
        out_ref[pl.ds(b, 8, blocks), :] = total[:, 128 * b : 128 * b + 128]
    for b in range(blocks // 4):
        at = inner + 128 * b
        out_ref[pl.ds(8 * blocks + b, 8, blocks // 4), :] = total[:, at : at + 128]


def project_kernel(w_ref, x0_ref, x1_ref, x2_ref, x3_ref, out_ref, tail_ref):
    far = w_ref.shape[0] // 8
    inner = x0_ref.shape[1]
    quarter = inner // 4
    for r, x_ref in enumerate((x0_ref, x1_ref, x2_ref, x3_ref)):
        out_ref[r, : 8 * far, :] = dot(w_ref[:, :inner], x_ref[...], NT)
        tail = None
        for q in range(4):
            tail_ref[r, q] = dot(w_ref[:, inner:], x_ref[:, q * quarter : (q + 1) * quarter], NT)
            part = tail_ref[r, q, pl.ds(q, 2 * far, 4), :]
            tail = part if tail is None else tail + part
        out_ref[r, 8 * far :, :] = tail


def as_column(row):
    n = row.shape[1]
    at = lax.broadcasted_iota(jnp.int32, (n, n), 0) == lax.broadcasted_iota(jnp.int32, (n, n), 1)
    return jnp.sum(jnp.where(at, jnp.broadcast_to(row, (n, n)), 0.0), axis=1, keepdims=True)


def bias_kernel(bias_ref, out_ref):
    out_ref[...] = jnp.broadcast_to(as_column(bias_ref[...]), out_ref.shape)


def rate_kernel(rate_ref, out_ref):
    out_ref[...] = jnp.broadcast_to(as_column(jnp.exp(rate_ref[...])), out_ref.shape)


def core_kernel(
    side, tp_ref, gain_ref, group_ref, rate_ref, bias_ref, g_ref, x_ref,
    pack_ref, gx_ref, proj_ref,
    cum_ref, cols_ref, row_ref, col_ref, scores_ref,
):
    heads = rate_ref.shape[0]
    t = g_ref.shape[0]
    near, rows, _ = group_ref.shape
    far = rows // 10
    for m in range(near):
        for f in range(far):
            at = natural(side, m, f)
            proj_ref[at : at + 8, :] = group_ref[m, 8 * f : 8 * f + 8, :]
            last = 8 * far + 2 * f
            proj_ref[at + 8 : at + 10, :] = group_ref[m, last : last + 2, :]
    raw = proj_ref[pl.ds(pl.multiple_of(2 * STATE + tp_ref[0] * heads, heads), heads), :]
    z = raw + bias_ref[...]
    rate = rate_ref[...]
    step = jnp.maximum(z, 0.0) + jnp.log1p(jnp.exp(-jnp.abs(z)))
    first = lax.broadcasted_iota(jnp.int32, (t, t), 0)
    second = lax.broadcasted_iota(jnp.int32, (t, t), 1)
    cum = dot(-step * rate, jnp.where(first <= second, 1.0, 0.0), NN, HIGHEST)
    cum_ref[...] = cum
    cols_ref[...] = jnp.transpose(
        jnp.concatenate([cum, step, jnp.zeros((t - 2 * heads, t), F32)], axis=0)
    )
    scores = dot(jnp.transpose(proj_ref[:STATE, :]), proj_ref[STATE : 2 * STATE, :], NN, HIGHEST)
    causal = first <= second
    scores_ref[...] = jnp.where(causal, scores, 0.0)
    pack_ref[:t, :] = jnp.zeros((t, t), F32)
    left = second < HEAD_DIM

    def pair(k, carry):
        lanes = pl.ds(pl.multiple_of(k * 2 * HEAD_DIM, 2 * HEAD_DIM), 2 * HEAD_DIM)
        g = g_ref[:, lanes]
        x = x_ref[:, lanes]
        cols = cols_ref[...]
        none = jnp.zeros_like(g)
        gs = (jnp.where(left, g, none), jnp.where(left, none, g))
        moved = jnp.zeros((t, 2 * HEAD_DIM), F32)
        for a in range(2):
            h = 2 * k + a
            product = dot(x, gs[a], NT)
            step_col = cols[:, heads + a : heads + a + 1]
            decay = jnp.exp(jnp.minimum(cum_ref[pl.ds(h, 1), :] - cols[:, a : a + 1], 0.0))
            faded = product * decay
            stepped = faded * step_col
            pack_ref[:t, :] += stepped
            col_ref[...] = jnp.where(
                second == h,
                jnp.sum(faded * scores_ref[...], axis=1, keepdims=True),
                col_ref[...],
            )
            row_ref[pl.ds(h, 1), :] = jnp.sum(stepped * scores_ref[...], axis=0, keepdims=True)
            moved += dot((decay * scores_ref[...]).astype(BF16), gs[a], NN)
        step_both = jnp.where(left, cols[:, heads : heads + 1], cols[:, heads + 1 : heads + 2])
        gain = jnp.where(left, gain_ref[0, 2 * k], gain_ref[0, 2 * k + 1])
        up = g.astype(F32)
        gx_ref[:, lanes] = up + (moved * step_both + gain * up)
        cols_ref[...] = pltpu.roll(cols, t - 2, 1)
        return carry

    lax.fori_loop(0, heads // 2, pair, 0)
    pack_ref[:t, :] = jnp.where(causal, pack_ref[:t, :], 0.0)
    col = jnp.transpose(col_ref[...])[:heads, :]
    dcum = row_ref[...] - step * col
    decayed = dot(dcum, jnp.where(first >= second, 1.0, 0.0), NN, HIGHEST)
    pack_ref[t:, :] = (col - rate * decayed) * (1.0 / (1.0 + jnp.exp(-z)))


def grads_kernel(side, pack_ref, proj_ref, send_ref, grad_ref, rows_ref):
    parts, rows, t = pack_ref.shape
    heads = rows - t
    scores = pack_ref[0, :t, :]
    for p in range(1, parts):
        scores = scores + pack_ref[p, :t, :]
    grad_ref[:STATE, :] = dot(proj_ref[STATE : 2 * STATE, :], scores, NT, HIGHEST)
    grad_ref[STATE : 2 * STATE, :] = dot(proj_ref[:STATE, :], scores, NN, HIGHEST)
    for p in range(parts):
        grad_ref[2 * STATE + p * heads : 2 * STATE + (p + 1) * heads, :] = pack_ref[p, t:, :]
    near, rows, _ = send_ref.shape
    far = rows // 10
    for m in range(near):
        for f in range(far):
            at = natural(side, m, f)
            rows_ref[m, 8 * f : 8 * f + 8, :] = grad_ref[at : at + 8, :]
            last = 8 * far + 2 * f
            rows_ref[m, last : last + 2, :] = grad_ref[at + 8 : at + 10, :]
    send_ref[...] = rows_ref[...].astype(BF16)


def weight_kernel(who_ref, grad_ref, x0_ref, x1_ref, x2_ref, x3_ref, out_ref, wide_ref):
    far = grad_ref.shape[1] // 10
    inner = x0_ref.shape[1]
    quarter = inner // 4
    main = tail = 0.0
    for r, x_ref in enumerate((x0_ref, x1_ref, x2_ref, x3_ref)):
        grad = grad_ref[who_ref[r]]
        main = main + dot(grad[: 8 * far, :], x_ref[...])
        for q in range(4):
            wide_ref[r, pl.ds(q, 2 * far, 4), :] = grad[8 * far :, :].astype(F32)
        wide = wide_ref[r]
        quarter_of = lax.broadcasted_iota(jnp.int32, wide.shape, 0) % 4
        for q in range(4):
            piece = jnp.where(quarter_of == q, wide, 0.0).astype(BF16)
            tail = tail + dot(piece, x_ref[:, q * quarter : (q + 1) * quarter])
    out_ref[:, :inner] = main.astype(BF16)
    out_ref[:, inner:] = tail.astype(BF16)


def back_kernel(who_ref, grad_ref, w0_ref, w1_ref, w2_ref, w3_ref, gx_ref, out_ref, wide_ref):
    far = grad_ref.shape[1] // 10
    inner = gx_ref.shape[1]
    quarter = inner // 4
    w_refs = (w0_ref, w1_ref, w2_ref, w3_ref)
    mains, tails = [], []
    for r in range(4):
        grad = grad_ref[who_ref[r]].astype(F32)
        mains.append(jnp.transpose(grad[: 8 * far, :]).astype(BF16))
        for q in range(4):
            wide_ref[r, pl.ds(q, 2 * far, 4), :] = grad[8 * far :, :]
        tails.append(jnp.transpose(wide_ref[r]))
    quarter_of = lax.broadcasted_iota(jnp.int32, tails[0].shape, 1) % 4
    for q in range(4):
        lanes = slice(q * quarter, (q + 1) * quarter)
        back = 0.0
        for r in range(4):
            piece = jnp.where(quarter_of == q, tails[r], 0.0).astype(BF16)
            back = back + (dot(mains[r], w_refs[r][:, lanes]) + dot(piece, w_refs[r][:, inner:]))
        out_ref[:, lanes] = (gx_ref[:, lanes] + back).astype(BF16)


NEAR = ("xl", "zl")
FAR = ("xh", "zh")
ROWS = ("xh", "xl", "zh", "zl")


def from_near(value, r):
    return lax.ppermute(value, NEAR, [(m, m ^ r) for m in range(lax.axis_size(NEAR))])


def per_device(saved_inputs, returned, proj_weight, log_rate, step_bias, skip_gain):
    x = saved_inputs[0]
    t, inner = x.shape
    heads = log_rate.shape[1]
    sections = lax.axis_size("pp")
    near = lax.axis_size(NEAR)
    far = lax.axis_size(FAR)
    side = lax.axis_size(("xh", "xl"))
    tps = lax.axis_size("tp")
    pcols = proj_weight.shape[2] * near * far
    rows = pcols // near
    wide = inner + 2 * inner // 8
    who = lax.axis_index(NEAR) ^ jnp.arange(near, dtype=jnp.int32)
    xs = [x] + [from_near(x, r) for r in range(1, near)]
    arrived = lax.ppermute(returned, "pp", [(i, (i - 1) % sections) for i in range(sections)])[0]
    rates = call(rate_kernel, jax.ShapeDtypeStruct((heads, t), F32), inputs=1)(log_rate)
    biases = call(bias_kernel, jax.ShapeDtypeStruct((heads, t), F32), inputs=1)(step_bias)

    spread_shard = call(
        shard_kernel,
        jax.ShapeDtypeStruct((far, 8, wide), BF16),
        scratch=[pltpu.VMEM((8, wide), F32)],
        inputs=1,
    )(proj_weight[0].T)
    weight = lax.all_to_all(spread_shard, FAR, 0, 0).reshape(far * 8, wide)
    diagonal = from_near(weight, 3)
    weights = [weight, from_near(weight, 1), from_near(weight, 2), diagonal]

    partial = call(
        project_kernel,
        jax.ShapeDtypeStruct((near, rows, t), F32),
        scratch=[pltpu.VMEM((near, 4, far * 8, t), F32)],
        inputs=5,
    )(weight, *xs)
    share = lax.all_to_all(partial, "tp", 0, 0).sum(axis=0)
    own = lax.ppermute(
        share,
        NEAR + ("tp",),
        [(m * tps + k, (m ^ k) * tps + m) for m in range(near) for k in range(tps)],
    )
    proj = lax.all_gather(own, "tp", axis=0)

    pack, gx, proj = call(
        functools.partial(core_kernel, side),
        (
            jax.ShapeDtypeStruct((t + heads, t), F32),
            jax.ShapeDtypeStruct((t, inner), F32),
            jax.ShapeDtypeStruct((pcols, t), F32),
        ),
        scratch=[
            pltpu.VMEM((heads, t), F32),
            pltpu.VMEM((t, t), F32),
            pltpu.VMEM((heads, t), F32),
            pltpu.VMEM((t, t), F32),
            pltpu.VMEM((t, t), F32),
        ],
        smem=(0, 1),
        inputs=7,
    )(lax.axis_index("tp").reshape(1), skip_gain, proj, rates, biases, arrived, x)

    packs = lax.all_gather(pack, "tp", axis=0)
    send = call(
        functools.partial(grads_kernel, side),
        jax.ShapeDtypeStruct((near, rows, t), BF16),
        scratch=[pltpu.VMEM((pcols, t), F32), pltpu.VMEM((near, rows, t), F32)],
        inputs=2,
    )(packs, proj)
    grads = lax.all_to_all(send, NEAR, 0, 0)
    contrib = call(
        weight_kernel,
        jax.ShapeDtypeStruct((far * 8, wide), BF16),
        scratch=[pltpu.VMEM((near, far * 8, t), F32)],
        smem=(0,),
        inputs=6,
    )(who, grads, *xs)
    pieces = lax.all_to_all(contrib.reshape(far, 8, wide), FAR, 0, 0)
    grad_inputs = call(
        back_kernel,
        jax.ShapeDtypeStruct((t, inner), BF16),
        scratch=[pltpu.VMEM((near, far * 8, t), F32)],
        smem=(0,),
        inputs=7,
    )(who, send, *weights, gx)
    wgrad = call(
        total_kernel, jax.ShapeDtypeStruct((10 * inner // 128, 128), F32), inputs=1
    )(pieces)
    wgrad = wgrad.reshape(10, inner // 128, 128).transpose(1, 2, 0).reshape(inner, 10)
    return (grad_inputs[None], wgrad[None])


def solution(mesh):
    side = 8
    fine = Mesh(
        mesh.devices.reshape(mesh.shape["pp"], side // 2, 2, side // 2, 2, mesh.shape["tp"]),
        ("pp", "xh", "xl", "zh", "zl", "tp"),
    )
    rows = ROWS
    placed = (
        P("pp", rows, "tp"),
        P("pp", rows, "tp"),
        P("pp", "tp", rows),
        P("pp", "tp"),
        P("pp", "tp"),
        P("pp", "tp"),
    )
    return jax.shard_map(
        per_device,
        mesh=fine,
        in_specs=placed,
        out_specs=(P("pp", rows, "tp"), P("pp", "tp", rows)),
        check_vma=False,
    )
```

```python
import functools

import jax
import jax.numpy as jnp
from jax import lax
from jax.experimental import pallas as pl
from jax.experimental.pallas import tpu as pltpu
from jax.sharding import Mesh, PartitionSpec as P


HEAD_DIM = 64
STATE = 256
F32 = jnp.float32
BF16 = jnp.bfloat16
HIGHEST = lax.Precision.HIGHEST
NT = (((1,), (1,)), ((), ()))
NN = (((1,), (0,)), ((), ()))
VMEM_LIMIT = 8 * 1024 * 1024


def dot(a, b, dims=NN, precision=None):
    return lax.dot_general(a, b, dims, precision=precision, preferred_element_type=F32)


def call(kernel, outs, scratch=(), smem=(), inputs=0):
    specs = [
        pl.BlockSpec(memory_space=pltpu.SMEM if i in smem else pltpu.VMEM) for i in range(inputs)
    ]
    return pl.pallas_call(
        kernel,
        out_shape=outs,
        in_specs=specs,
        out_specs=jax.tree.map(lambda _: pl.BlockSpec(memory_space=pltpu.VMEM), outs),
        scratch_shapes=list(scratch),
        compiler_params=pltpu.CompilerParams(vmem_limit_bytes=VMEM_LIMIT),
    )


def natural(side, m, f):
    half = side // 2
    return 10 * ((2 * (f // half) + m // 2) * side + 2 * (f % half) + m % 2)


def shard_kernel(w_ref, out_ref, row_ref):
    copies, _, _ = out_ref.shape
    inner = w_ref.shape[1]
    quarter = inner // 4
    w = w_ref[...].astype(F32)
    row_ref[:, :inner] = w[:8, :]
    for c in range(2):
        for q in range(4):
            row_ref[4 * c + q : 4 * c + q + 1, inner:] = w[
                8 + c : 9 + c, q * quarter : (q + 1) * quarter
            ]
    row = row_ref[...].astype(BF16)
    for i in range(copies):
        out_ref[i] = row


def total_kernel(piece_ref, out_ref):
    count, _, wide = piece_ref.shape
    blocks = wide // 160
    inner = blocks * 128
    total = piece_ref[0].astype(F32)
    for i in range(1, count):
        total = total + piece_ref[i].astype(F32)
    for b in range(blocks):
        out_ref[pl.ds(b, 8, blocks), :] = total[:, 128 * b : 128 * b + 128]
    for b in range(blocks // 4):
        at = inner + 128 * b
        out_ref[pl.ds(8 * blocks + b, 8, blocks // 4), :] = total[:, at : at + 128]


def project_kernel(who_ref, w_ref, x0_ref, x1_ref, x2_ref, x3_ref, out_ref, tail_ref):
    far = w_ref.shape[0] // 8
    inner = x0_ref.shape[1]
    quarter = inner // 4
    for r, x_ref in enumerate((x0_ref, x1_ref, x2_ref, x3_ref)):
        out_ref[who_ref[r], : 8 * far, :] = dot(w_ref[:, :inner], x_ref[...], NT)
        tail = None
        for q in range(4):
            tail_ref[r, q] = dot(w_ref[:, inner:], x_ref[:, q * quarter : (q + 1) * quarter], NT)
            part = tail_ref[r, q, pl.ds(q, 2 * far, 4), :]
            tail = part if tail is None else tail + part
        out_ref[who_ref[r], 8 * far :, :] = tail


def as_column(row):
    n = row.shape[1]
    at = lax.broadcasted_iota(jnp.int32, (n, n), 0) == lax.broadcasted_iota(jnp.int32, (n, n), 1)
    return jnp.sum(jnp.where(at, jnp.broadcast_to(row, (n, n)), 0.0), axis=1, keepdims=True)


def rate_kernel(rate_ref, bias_ref, gain_ref, out_ref, lanes_ref):
    _, heads, t = out_ref.shape
    out_ref[0] = jnp.broadcast_to(as_column(jnp.exp(rate_ref[...])), (heads, t))
    out_ref[1] = jnp.broadcast_to(as_column(bias_ref[...]), (heads, t))
    left = lax.broadcasted_iota(jnp.int32, (1, 2 * HEAD_DIM), 1) < HEAD_DIM
    for k in range(heads // 2):
        lanes_ref[:, 2 * HEAD_DIM * k : 2 * HEAD_DIM * (k + 1)] = jnp.where(
            left, gain_ref[:, 2 * k : 2 * k + 1], gain_ref[:, 2 * k + 1 : 2 * k + 2]
        )


def core_kernel(
    side, tp_ref, gain_ref, group_ref, head_ref, g_ref, x_ref,
    pack_ref, gx_ref, proj_ref,
    cum_ref, cols_ref, row_ref, col_ref, scores_ref,
):
    heads = head_ref.shape[1]
    t = g_ref.shape[0]
    near, rows, _ = group_ref.shape
    far = rows // 10
    for m in range(near):
        for f in range(far):
            at = natural(side, m, f)
            proj_ref[at : at + 8, :] = group_ref[m, 8 * f : 8 * f + 8, :]
            last = 8 * far + 2 * f
            proj_ref[at + 8 : at + 10, :] = group_ref[m, last : last + 2, :]
    raw = proj_ref[pl.ds(pl.multiple_of(2 * STATE + tp_ref[0] * heads, heads), heads), :]
    z = raw + head_ref[1]
    rate = head_ref[0]
    step = jnp.maximum(z, 0.0) + jnp.log1p(jnp.exp(-jnp.abs(z)))
    first = lax.broadcasted_iota(jnp.int32, (t, t), 0)
    second = lax.broadcasted_iota(jnp.int32, (t, t), 1)
    cum = dot(-step * rate, jnp.where(first <= second, 1.0, 0.0), NN, HIGHEST)
    cum_ref[...] = cum
    cols_ref[...] = jnp.transpose(
        jnp.concatenate([cum, step, jnp.zeros((t - 2 * heads, t), F32)], axis=0)
    )
    scores = dot(jnp.transpose(proj_ref[:STATE, :]), proj_ref[STATE : 2 * STATE, :], NN, HIGHEST)
    causal = first <= second
    scores_ref[...] = jnp.where(causal, scores, 0.0)
    pack_ref[:t, :] = jnp.zeros((t, t), F32)
    left = second < HEAD_DIM

    def pair(k, carry):
        lanes = pl.ds(pl.multiple_of(k * 2 * HEAD_DIM, 2 * HEAD_DIM), 2 * HEAD_DIM)
        g = g_ref[:, lanes]
        x = x_ref[:, lanes]
        cols = cols_ref[...]
        none = jnp.zeros_like(g)
        gs = (jnp.where(left, g, none), jnp.where(left, none, g))
        moved = jnp.zeros((t, 2 * HEAD_DIM), F32)
        for a in range(2):
            h = 2 * k + a
            product = dot(x, gs[a], NT)
            step_col = cols[:, heads + a : heads + a + 1]
            decay = jnp.exp(jnp.minimum(cum_ref[pl.ds(h, 1), :] - cols[:, a : a + 1], 0.0))
            faded = product * decay
            stepped = faded * step_col
            pack_ref[:t, :] += stepped
            col_ref[...] = jnp.where(
                second == h,
                jnp.sum(faded * scores_ref[...], axis=1, keepdims=True),
                col_ref[...],
            )
            row_ref[pl.ds(h, 1), :] = jnp.sum(stepped * scores_ref[...], axis=0, keepdims=True)
            moved += dot((decay * scores_ref[...]).astype(BF16), gs[a], NN)
        step_both = jnp.where(left, cols[:, heads : heads + 1], cols[:, heads + 1 : heads + 2])
        gain = gain_ref[:, lanes]
        up = g.astype(F32)
        gx_ref[:, lanes] = up + (moved * step_both + gain * up)
        cols_ref[...] = pltpu.roll(cols, t - 2, 1)
        return carry

    lax.fori_loop(0, heads // 2, pair, 0)
    pack_ref[:t, :] = jnp.where(causal, pack_ref[:t, :], 0.0)
    col = jnp.transpose(col_ref[...])[:heads, :]
    dcum = row_ref[...] - step * col
    decayed = dot(dcum, jnp.where(first >= second, 1.0, 0.0), NN, HIGHEST)
    pack_ref[t:, :] = (col - rate * decayed) * (1.0 / (1.0 + jnp.exp(-z)))


def grads_kernel(side, pack_ref, proj_ref, send_ref, grad_ref, rows_ref):
    parts, rows, t = pack_ref.shape
    heads = rows - t
    scores = pack_ref[0, :t, :]
    for p in range(1, parts):
        scores = scores + pack_ref[p, :t, :]
    grad_ref[:STATE, :] = dot(proj_ref[STATE : 2 * STATE, :], scores, NT, HIGHEST)
    grad_ref[STATE : 2 * STATE, :] = dot(proj_ref[:STATE, :], scores, NN, HIGHEST)
    for p in range(parts):
        grad_ref[2 * STATE + p * heads : 2 * STATE + (p + 1) * heads, :] = pack_ref[p, t:, :]
    near, rows, _ = send_ref.shape
    far = rows // 10
    for m in range(near):
        for f in range(far):
            at = natural(side, m, f)
            rows_ref[m, 8 * f : 8 * f + 8, :] = grad_ref[at : at + 8, :]
            last = 8 * far + 2 * f
            rows_ref[m, last : last + 2, :] = grad_ref[at + 8 : at + 10, :]
    send_ref[...] = rows_ref[...].astype(BF16)


def weight_kernel(who_ref, grad_ref, x0_ref, x1_ref, x2_ref, x3_ref, out_ref, wide_ref):
    far = grad_ref.shape[1] // 10
    inner = x0_ref.shape[1]
    quarter = inner // 4
    main = tail = 0.0
    for r, x_ref in enumerate((x0_ref, x1_ref, x2_ref, x3_ref)):
        grad = grad_ref[who_ref[r]]
        main = main + dot(grad[: 8 * far, :], x_ref[...])
        for q in range(4):
            wide_ref[r, pl.ds(q, 2 * far, 4), :] = grad[8 * far :, :].astype(F32)
        wide = wide_ref[r]
        quarter_of = lax.broadcasted_iota(jnp.int32, wide.shape, 0) % 4
        for q in range(4):
            piece = jnp.where(quarter_of == q, wide, 0.0).astype(BF16)
            tail = tail + dot(piece, x_ref[:, q * quarter : (q + 1) * quarter])
    out_ref[:, :inner] = main.astype(BF16)
    out_ref[:, inner:] = tail.astype(BF16)


def back_kernel(who_ref, grad_ref, w0_ref, w1_ref, w2_ref, w3_ref, gx_ref, out_ref, wide_ref):
    far = grad_ref.shape[1] // 10
    inner = gx_ref.shape[1]
    quarter = inner // 4
    w_refs = (w0_ref, w1_ref, w2_ref, w3_ref)
    mains, tails = [], []
    for r in range(4):
        grad = grad_ref[who_ref[r]].astype(F32)
        mains.append(jnp.transpose(grad[: 8 * far, :]).astype(BF16))
        for q in range(4):
            wide_ref[r, pl.ds(q, 2 * far, 4), :] = grad[8 * far :, :]
        tails.append(jnp.transpose(wide_ref[r]))
    quarter_of = lax.broadcasted_iota(jnp.int32, tails[0].shape, 1) % 4
    for q in range(4):
        lanes = slice(q * quarter, (q + 1) * quarter)
        back = 0.0
        for r in range(4):
            piece = jnp.where(quarter_of == q, tails[r], 0.0).astype(BF16)
            back = back + (dot(mains[r], w_refs[r][:, lanes]) + dot(piece, w_refs[r][:, inner:]))
        out_ref[:, lanes] = (gx_ref[:, lanes] + back).astype(BF16)


NEAR = ("xl", "zl")
FAR = ("xh", "zh")
ROWS = ("xh", "xl", "zh", "zl")


def from_near(value, r):
    return lax.ppermute(value, NEAR, [(m, m ^ r) for m in range(lax.axis_size(NEAR))])


def per_device(saved_inputs, returned, proj_weight, log_rate, step_bias, skip_gain):
    x = saved_inputs[0]
    t, inner = x.shape
    heads = log_rate.shape[1]
    sections = lax.axis_size("pp")
    near = lax.axis_size(NEAR)
    far = lax.axis_size(FAR)
    side = lax.axis_size(("xh", "xl"))
    pcols = proj_weight.shape[2] * near * far
    rows = pcols // near
    wide = inner + 2 * inner // 8
    who = lax.axis_index(NEAR) ^ jnp.arange(near, dtype=jnp.int32)
    xs = [x] + [from_near(x, r) for r in range(1, near)]
    arrived = lax.ppermute(returned, "pp", [(i, (i - 1) % sections) for i in range(sections)])[0]
    of_heads, gains = call(
        rate_kernel,
        (
            jax.ShapeDtypeStruct((2, heads, t), F32),
            jax.ShapeDtypeStruct((1, inner), F32),
        ),
        inputs=3,
    )(log_rate, step_bias, skip_gain)

    spread_shard = call(
        shard_kernel,
        jax.ShapeDtypeStruct((far, 8, wide), BF16),
        scratch=[pltpu.VMEM((8, wide), F32)],
        inputs=1,
    )(proj_weight[0].T)
    weight = lax.all_to_all(spread_shard, FAR, 0, 0).reshape(far * 8, wide)
    weights = [weight] + [from_near(weight, r) for r in range(1, near)]

    partial = call(
        project_kernel,
        jax.ShapeDtypeStruct((near, rows, t), F32),
        scratch=[pltpu.VMEM((near, 4, far * 8, t), F32)],
        smem=(0,),
        inputs=6,
    )(who, weight, *xs)
    partial = lax.all_to_all(partial, NEAR, 0, 0)
    own = lax.all_to_all(partial, "tp", 0, 0).sum(axis=0)
    proj = lax.all_gather(own, "tp", axis=0)

    pack, gx, proj = call(
        functools.partial(core_kernel, side),
        (
            jax.ShapeDtypeStruct((t + heads, t), F32),
            jax.ShapeDtypeStruct((t, inner), F32),
            jax.ShapeDtypeStruct((pcols, t), F32),
        ),
        scratch=[
            pltpu.VMEM((heads, t), F32),
            pltpu.VMEM((t, t), F32),
            pltpu.VMEM((heads, t), F32),
            pltpu.VMEM((t, t), F32),
            pltpu.VMEM((t, t), F32),
        ],
        smem=(0,),
        inputs=6,
    )(lax.axis_index("tp").reshape(1), gains, proj, of_heads, arrived, x)

    packs = lax.all_gather(pack, "tp", axis=0)
    send = call(
        functools.partial(grads_kernel, side),
        jax.ShapeDtypeStruct((near, rows, t), BF16),
        scratch=[pltpu.VMEM((pcols, t), F32), pltpu.VMEM((near, rows, t), F32)],
        inputs=2,
    )(packs, proj)
    grads = lax.all_to_all(send, NEAR, 0, 0)
    contrib = call(
        weight_kernel,
        jax.ShapeDtypeStruct((far * 8, wide), BF16),
        scratch=[pltpu.VMEM((near, far * 8, t), F32)],
        smem=(0,),
        inputs=6,
    )(who, grads, *xs)
    pieces = lax.all_to_all(contrib.reshape(far, 8, wide), FAR, 0, 0)
    grad_inputs = call(
        back_kernel,
        jax.ShapeDtypeStruct((t, inner), BF16),
        scratch=[pltpu.VMEM((near, far * 8, t), F32)],
        smem=(0,),
        inputs=7,
    )(who, send, *weights, gx)
    wgrad = call(
        total_kernel, jax.ShapeDtypeStruct((10 * inner // 128, 128), F32), inputs=1
    )(pieces)
    wgrad = wgrad.reshape(10, inner // 128, 128).transpose(1, 2, 0).reshape(inner, 10)
    return (grad_inputs[None], wgrad[None])


def solution(mesh):
    side = 8
    fine = Mesh(
        mesh.devices.reshape(mesh.shape["pp"], side // 2, 2, side // 2, 2, mesh.shape["tp"]),
        ("pp", "xh", "xl", "zh", "zl", "tp"),
    )
    rows = ROWS
    placed = (
        P("pp", rows, "tp"),
        P("pp", rows, "tp"),
        P("pp", "tp", rows),
        P("pp", "tp"),
        P("pp", "tp"),
        P("pp", "tp"),
    )
    return jax.shard_map(
        per_device,
        mesh=fine,
        in_specs=placed,
        out_specs=(P("pp", rows, "tp"), P("pp", "tp", rows)),
        check_vma=False,
    )
```

```python
import functools

import jax
import jax.numpy as jnp
from jax import lax
from jax.experimental import pallas as pl
from jax.experimental.pallas import tpu as pltpu
from jax.sharding import Mesh, PartitionSpec as P


HEAD_DIM = 64
STATE = 256
F32 = jnp.float32
BF16 = jnp.bfloat16
HIGHEST = lax.Precision.HIGHEST
NT = (((1,), (1,)), ((), ()))
NN = (((1,), (0,)), ((), ()))
VMEM_LIMIT = 8 * 1024 * 1024


def dot(a, b, dims=NN, precision=None):
    return lax.dot_general(a, b, dims, precision=precision, preferred_element_type=F32)


def call(kernel, outs, scratch=(), smem=(), inputs=0):
    specs = [
        pl.BlockSpec(memory_space=pltpu.SMEM if i in smem else pltpu.VMEM) for i in range(inputs)
    ]
    return pl.pallas_call(
        kernel,
        out_shape=outs,
        in_specs=specs,
        out_specs=jax.tree.map(lambda _: pl.BlockSpec(memory_space=pltpu.VMEM), outs),
        scratch_shapes=list(scratch),
        compiler_params=pltpu.CompilerParams(vmem_limit_bytes=VMEM_LIMIT),
    )


def natural(side, m, f):
    half = side // 2
    return 10 * ((2 * (f // half) + m // 2) * side + 2 * (f % half) + m % 2)


def shard_kernel(w_ref, out_ref, row_ref):
    copies, _, _ = out_ref.shape
    inner = w_ref.shape[1]
    quarter = inner // 4
    w = w_ref[...].astype(F32)
    row_ref[:, :inner] = w[:8, :]
    for c in range(2):
        for q in range(4):
            row_ref[4 * c + q : 4 * c + q + 1, inner:] = w[
                8 + c : 9 + c, q * quarter : (q + 1) * quarter
            ]
    row = row_ref[...].astype(BF16)
    for i in range(copies):
        out_ref[i] = row


def total_kernel(piece_ref, out_ref):
    count, _, wide = piece_ref.shape
    blocks = wide // 160
    inner = blocks * 128
    total = piece_ref[0].astype(F32)
    for i in range(1, count):
        total = total + piece_ref[i].astype(F32)
    for b in range(blocks):
        out_ref[pl.ds(b, 8, blocks), :] = total[:, 128 * b : 128 * b + 128]
    for b in range(blocks // 4):
        at = inner + 128 * b
        out_ref[pl.ds(8 * blocks + b, 8, blocks // 4), :] = total[:, at : at + 128]


def project_kernel(who_ref, w_ref, x0_ref, x1_ref, x2_ref, x3_ref, out_ref, tail_ref):
    far = w_ref.shape[0] // 8
    inner = x0_ref.shape[1]
    quarter = inner // 4
    for r, x_ref in enumerate((x0_ref, x1_ref, x2_ref, x3_ref)):
        out_ref[who_ref[r], : 8 * far, :] = dot(w_ref[:, :inner], x_ref[...], NT)
        tail = None
        for q in range(4):
            tail_ref[r, q] = dot(w_ref[:, inner:], x_ref[:, q * quarter : (q + 1) * quarter], NT)
            part = tail_ref[r, q, pl.ds(q, 2 * far, 4), :]
            tail = part if tail is None else tail + part
        out_ref[who_ref[r], 8 * far :, :] = tail


def as_column(row):
    n = row.shape[1]
    at = lax.broadcasted_iota(jnp.int32, (n, n), 0) == lax.broadcasted_iota(jnp.int32, (n, n), 1)
    return jnp.sum(jnp.where(at, jnp.broadcast_to(row, (n, n)), 0.0), axis=1, keepdims=True)


def rate_kernel(rate_ref, bias_ref, out_ref):
    _, heads, t = out_ref.shape
    out_ref[0] = jnp.broadcast_to(as_column(jnp.exp(rate_ref[...])), (heads, t))
    out_ref[1] = jnp.broadcast_to(as_column(bias_ref[...]), (heads, t))


def gain_kernel(gain_ref, lanes_ref):
    heads = gain_ref.shape[1]
    left = lax.broadcasted_iota(jnp.int32, (1, 2 * HEAD_DIM), 1) < HEAD_DIM
    for k in range(heads // 2):
        lanes_ref[:, 2 * HEAD_DIM * k : 2 * HEAD_DIM * (k + 1)] = jnp.where(
            left, gain_ref[:, 2 * k : 2 * k + 1], gain_ref[:, 2 * k + 1 : 2 * k + 2]
        )


def core_kernel(
    side, tp_ref, gain_ref, group_ref, head_ref, g_ref, x_ref,
    pack_ref, gx_ref, proj_ref,
    cum_ref, cols_ref, row_ref, col_ref, scores_ref,
):
    heads = head_ref.shape[1]
    t = g_ref.shape[0]
    near, rows, _ = group_ref.shape
    far = rows // 10
    for m in range(near):
        for f in range(far):
            at = natural(side, m, f)
            proj_ref[at : at + 8, :] = group_ref[m, 8 * f : 8 * f + 8, :]
            last = 8 * far + 2 * f
            proj_ref[at + 8 : at + 10, :] = group_ref[m, last : last + 2, :]
    raw = proj_ref[pl.ds(pl.multiple_of(2 * STATE + tp_ref[0] * heads, heads), heads), :]
    z = raw + head_ref[1]
    rate = head_ref[0]
    step = jnp.maximum(z, 0.0) + jnp.log1p(jnp.exp(-jnp.abs(z)))
    first = lax.broadcasted_iota(jnp.int32, (t, t), 0)
    second = lax.broadcasted_iota(jnp.int32, (t, t), 1)
    cum = dot(-step * rate, jnp.where(first <= second, 1.0, 0.0), NN, HIGHEST)
    cum_ref[...] = cum
    cols_ref[...] = jnp.transpose(
        jnp.concatenate([cum, step, jnp.zeros((t - 2 * heads, t), F32)], axis=0)
    )
    scores = dot(jnp.transpose(proj_ref[:STATE, :]), proj_ref[STATE : 2 * STATE, :], NN, HIGHEST)
    causal = first <= second
    scores_ref[...] = jnp.where(causal, scores, 0.0)
    pack_ref[:t, :] = jnp.zeros((t, t), F32)
    left = second < HEAD_DIM

    def pair(k, carry):
        lanes = pl.ds(pl.multiple_of(k * 2 * HEAD_DIM, 2 * HEAD_DIM), 2 * HEAD_DIM)
        g = g_ref[:, lanes]
        x = x_ref[:, lanes]
        cols = cols_ref[...]
        none = jnp.zeros_like(g)
        gs = (jnp.where(left, g, none), jnp.where(left, none, g))
        moved = jnp.zeros((t, 2 * HEAD_DIM), F32)
        for a in range(2):
            h = 2 * k + a
            product = dot(x, gs[a], NT)
            step_col = cols[:, heads + a : heads + a + 1]
            decay = jnp.exp(jnp.minimum(cum_ref[pl.ds(h, 1), :] - cols[:, a : a + 1], 0.0))
            faded = product * decay
            stepped = faded * step_col
            pack_ref[:t, :] += stepped
            col_ref[...] = jnp.where(
                second == h,
                jnp.sum(faded * scores_ref[...], axis=1, keepdims=True),
                col_ref[...],
            )
            row_ref[pl.ds(h, 1), :] = jnp.sum(stepped * scores_ref[...], axis=0, keepdims=True)
            moved += dot((decay * scores_ref[...]).astype(BF16), gs[a], NN)
        step_both = jnp.where(left, cols[:, heads : heads + 1], cols[:, heads + 1 : heads + 2])
        gain = gain_ref[:, lanes]
        up = g.astype(F32)
        gx_ref[:, lanes] = up + (moved * step_both + gain * up)
        cols_ref[...] = pltpu.roll(cols, t - 2, 1)
        return carry

    lax.fori_loop(0, heads // 2, pair, 0)
    pack_ref[:t, :] = jnp.where(causal, pack_ref[:t, :], 0.0)
    col = jnp.transpose(col_ref[...])[:heads, :]
    dcum = row_ref[...] - step * col
    decayed = dot(dcum, jnp.where(first >= second, 1.0, 0.0), NN, HIGHEST)
    pack_ref[t:, :] = (col - rate * decayed) * (1.0 / (1.0 + jnp.exp(-z)))


def grads_kernel(side, pack_ref, proj_ref, send_ref, grad_ref, rows_ref):
    parts, rows, t = pack_ref.shape
    heads = rows - t
    scores = pack_ref[0, :t, :]
    for p in range(1, parts):
        scores = scores + pack_ref[p, :t, :]
    grad_ref[:STATE, :] = dot(proj_ref[STATE : 2 * STATE, :], scores, NT, HIGHEST)
    grad_ref[STATE : 2 * STATE, :] = dot(proj_ref[:STATE, :], scores, NN, HIGHEST)
    for p in range(parts):
        grad_ref[2 * STATE + p * heads : 2 * STATE + (p + 1) * heads, :] = pack_ref[p, t:, :]
    near, rows, _ = send_ref.shape
    far = rows // 10
    for m in range(near):
        for f in range(far):
            at = natural(side, m, f)
            rows_ref[m, 8 * f : 8 * f + 8, :] = grad_ref[at : at + 8, :]
            last = 8 * far + 2 * f
            rows_ref[m, last : last + 2, :] = grad_ref[at + 8 : at + 10, :]
    send_ref[...] = rows_ref[...].astype(BF16)


def weight_kernel(who_ref, grad_ref, x0_ref, x1_ref, x2_ref, x3_ref, out_ref, wide_ref):
    far = grad_ref.shape[1] // 10
    inner = x0_ref.shape[1]
    quarter = inner // 4
    main = tail = 0.0
    for r, x_ref in enumerate((x0_ref, x1_ref, x2_ref, x3_ref)):
        grad = grad_ref[who_ref[r]]
        main = main + dot(grad[: 8 * far, :], x_ref[...])
        for q in range(4):
            wide_ref[r, pl.ds(q, 2 * far, 4), :] = grad[8 * far :, :].astype(F32)
        wide = wide_ref[r]
        quarter_of = lax.broadcasted_iota(jnp.int32, wide.shape, 0) % 4
        for q in range(4):
            piece = jnp.where(quarter_of == q, wide, 0.0).astype(BF16)
            tail = tail + dot(piece, x_ref[:, q * quarter : (q + 1) * quarter])
    out_ref[:, :inner] = main.astype(BF16)
    out_ref[:, inner:] = tail.astype(BF16)


def back_kernel(who_ref, grad_ref, w0_ref, w1_ref, w2_ref, w3_ref, gx_ref, out_ref, wide_ref):
    far = grad_ref.shape[1] // 10
    inner = gx_ref.shape[1]
    quarter = inner // 4
    w_refs = (w0_ref, w1_ref, w2_ref, w3_ref)
    mains, tails = [], []
    for r in range(4):
        grad = grad_ref[who_ref[r]].astype(F32)
        mains.append(jnp.transpose(grad[: 8 * far, :]).astype(BF16))
        for q in range(4):
            wide_ref[r, pl.ds(q, 2 * far, 4), :] = grad[8 * far :, :]
        tails.append(jnp.transpose(wide_ref[r]))
    quarter_of = lax.broadcasted_iota(jnp.int32, tails[0].shape, 1) % 4
    for q in range(4):
        lanes = slice(q * quarter, (q + 1) * quarter)
        back = 0.0
        for r in range(4):
            piece = jnp.where(quarter_of == q, tails[r], 0.0).astype(BF16)
            back = back + (dot(mains[r], w_refs[r][:, lanes]) + dot(piece, w_refs[r][:, inner:]))
        out_ref[:, lanes] = (gx_ref[:, lanes] + back).astype(BF16)


NEAR = ("xl", "zl")
FAR = ("xh", "zh")
ROWS = ("xh", "xl", "zh", "zl")


def from_near(value, r):
    return lax.ppermute(value, NEAR, [(m, m ^ r) for m in range(lax.axis_size(NEAR))])


def per_device(saved_inputs, returned, proj_weight, log_rate, step_bias, skip_gain):
    x = saved_inputs[0]
    t, inner = x.shape
    heads = log_rate.shape[1]
    sections = lax.axis_size("pp")
    near = lax.axis_size(NEAR)
    far = lax.axis_size(FAR)
    side = lax.axis_size(("xh", "xl"))
    pcols = proj_weight.shape[2] * near * far
    rows = pcols // near
    wide = inner + 2 * inner // 8
    who = lax.axis_index(NEAR) ^ jnp.arange(near, dtype=jnp.int32)
    xs = [x] + [from_near(x, r) for r in range(1, near)]
    arrived = lax.ppermute(returned, "pp", [(i, (i - 1) % sections) for i in range(sections)])[0]
    of_heads = call(
        rate_kernel, jax.ShapeDtypeStruct((2, heads, t), F32), inputs=2
    )(log_rate, step_bias)
    gains = call(gain_kernel, jax.ShapeDtypeStruct((1, inner), F32), inputs=1)(skip_gain)

    spread_shard = call(
        shard_kernel,
        jax.ShapeDtypeStruct((far, 8, wide), BF16),
        scratch=[pltpu.VMEM((8, wide), F32)],
        inputs=1,
    )(proj_weight[0].T)
    weight = lax.all_to_all(spread_shard, FAR, 0, 0).reshape(far * 8, wide)
    diagonal = from_near(weight, 3)
    weights = [weight, from_near(weight, 1), from_near(weight, 2), diagonal]

    partial = call(
        project_kernel,
        jax.ShapeDtypeStruct((near, rows, t), F32),
        scratch=[pltpu.VMEM((near, 4, far * 8, t), F32)],
        smem=(0,),
        inputs=6,
    )(who, weight, *xs)
    partial = lax.all_to_all(partial, NEAR, 0, 0)
    own = lax.all_to_all(partial, "tp", 0, 0).sum(axis=0)
    proj = lax.all_gather(own, "tp", axis=0)

    pack, gx, proj = call(
        functools.partial(core_kernel, side),
        (
            jax.ShapeDtypeStruct((t + heads, t), F32),
            jax.ShapeDtypeStruct((t, inner), F32),
            jax.ShapeDtypeStruct((pcols, t), F32),
        ),
        scratch=[
            pltpu.VMEM((heads, t), F32),
            pltpu.VMEM((t, t), F32),
            pltpu.VMEM((heads, t), F32),
            pltpu.VMEM((t, t), F32),
            pltpu.VMEM((t, t), F32),
        ],
        smem=(0,),
        inputs=6,
    )(lax.axis_index("tp").reshape(1), gains, proj, of_heads, arrived, x)

    packs = lax.all_gather(pack, "tp", axis=0)
    send = call(
        functools.partial(grads_kernel, side),
        jax.ShapeDtypeStruct((near, rows, t), BF16),
        scratch=[pltpu.VMEM((pcols, t), F32), pltpu.VMEM((near, rows, t), F32)],
        inputs=2,
    )(packs, proj)
    grads = lax.all_to_all(send, NEAR, 0, 0)
    contrib = call(
        weight_kernel,
        jax.ShapeDtypeStruct((far * 8, wide), BF16),
        scratch=[pltpu.VMEM((near, far * 8, t), F32)],
        smem=(0,),
        inputs=6,
    )(who, grads, *xs)
    pieces = lax.all_to_all(contrib.reshape(far, 8, wide), FAR, 0, 0)
    grad_inputs = call(
        back_kernel,
        jax.ShapeDtypeStruct((t, inner), BF16),
        scratch=[pltpu.VMEM((near, far * 8, t), F32)],
        smem=(0,),
        inputs=7,
    )(who, send, *weights, gx)
    wgrad = call(
        total_kernel, jax.ShapeDtypeStruct((10 * inner // 128, 128), F32), inputs=1
    )(pieces)
    wgrad = wgrad.reshape(10, inner // 128, 128).transpose(1, 2, 0).reshape(inner, 10)
    return (grad_inputs[None], wgrad[None])


def solution(mesh):
    side = 8
    fine = Mesh(
        mesh.devices.reshape(mesh.shape["pp"], side // 2, 2, side // 2, 2, mesh.shape["tp"]),
        ("pp", "xh", "xl", "zh", "zl", "tp"),
    )
    rows = ROWS
    placed = (
        P("pp", rows, "tp"),
        P("pp", rows, "tp"),
        P("pp", "tp", rows),
        P("pp", "tp"),
        P("pp", "tp"),
        P("pp", "tp"),
    )
    return jax.shard_map(
        per_device,
        mesh=fine,
        in_specs=placed,
        out_specs=(P("pp", rows, "tp"), P("pp", "tp", rows)),
        check_vma=False,
    )
```
